1024 devices in a mesh: wave: 64 (over y_lo, x, core), lev: 16 (over y_hi, z).
Axes of the slice: x: 8, y: 8 (y_hi: 2, y_lo: 4; y = y_hi * 4 + y_lo), z: 8, core: 2. Of those that a mesh axis runs over, the one named last changes fastest.
Arguments:
- vort_div: float32 [4, 16, 640, 640], P(None, 'lev', 'wave'), may hold values from -0.4 to 0.4
- legendre: float32 [640, 64, 640], P('wave'), may hold values from -0.3125 to 0.3125
- owner_map: int32 [640], replicated, may hold values from 0 to 639, as said below
- lat_sine: float32 [64], P('wave'), may hold values from -0.9 to 0.9
- quad_weight: float32 [64], P('wave'), may hold values from 2 to 6
- thickness: float32 [16], P('lev'), may hold values from 0.02 to 0.08
- tracers: float32 [8, 16, 64, 1280], P(None, 'lev', 'wave'), may hold values from -6 to 6
Outputs:
- tendency: float32 [8, 2, 16, 640, 640], P(None, None, 'lev', 'wave')
The draws below stay inside these ranges and needn't reach their ends.
Inputs may be any that keep to these rules, and one draw needn't show every extreme that they name: `owner_map`: a permutation of the 640 wavenumbers in which slots 2 i and 2 i + 1 hold m and 639 - m.
All inputs are finite; a program needn't handle non-finite values.
Results may differ from the reference program's by a relative error of at most 0.00007.
Values sent between devices are 32-bit elements; how exact they have to be, the bound alone decides.
No kernel may reach another device: no remote copies, remote signals or barrier semaphores. Data moves between devices by JAX's collectives and lax.ppermute only.
A program may use at most 32 MiB of HBM per device.

```python
import math
import jax
import jax.numpy as jnp
from jax import lax

M = 640
NLON = 1280
LATS = 64
LEVELS = 16
TRACERS = 8


def draw_owner_map(key, part):
    shuffled = jax.random.permutation(jax.random.fold_in(key, 17), M // 2)
    paired = jnp.stack([shuffled, M - 1 - shuffled], axis=1).reshape(-1)
    return paired.astype(jnp.int32)


def level_of(stream_key, dims, cuts, low, top_value):
    factor_of, own = 1.0, jax.random.fold_in(stream_key, 6)
    for axis_at, parts in cuts:
        draws = jnp.exp(jax.random.uniform(jax.random.fold_in(own, axis_at), (parts,), jnp.float32, low / len(cuts), top_value / len(cuts)))
        factor_of = factor_of * jnp.repeat(draws, dims[axis_at] // parts).reshape([-1 if axis == axis_at else 1 for axis in range(len(dims))])
    return factor_of


def scatter_about(key, shape, spread, most, shards=(), kind=jnp.bfloat16):
    drawn = jax.random.normal(key, shape, jnp.float32) * spread
    if len(shards) > 0:
        drawn = level_of(key, shape, shards, -0.22, 0.18) * drawn
    return jnp.clip(drawn, min=-most, max=most).astype(kind)


def setup_inputs(seed: int = 0) -> dict:
    keys = jax.random.split(jax.random.key(seed), 8)
    vort_div = scatter_about(keys[0], (4, LEVELS, M, M), 0.05, 0.4, ((1, 16), (2, 64)), jnp.float32)
    legendre = scatter_about(keys[1], (M, LATS, M), (M // 2) ** -0.5, 0.3125, ((0, 64),), jnp.float32)
    owner_map = draw_owner_map(jax.random.fold_in(keys[7], 71), 0)
    lat_sine = jnp.clip(jax.random.uniform(keys[3], (LATS,), jnp.float32, -0.9, 0.9) * level_of(keys[3], (LATS,), ((0, 64),), -0.4, 0.0), -0.9, 0.9)
    quad_weight = jnp.clip(2.0 + 4.0 * jax.random.uniform(keys[4], (LATS,), jnp.float32) ** level_of(keys[4], (LATS,), ((0, 64),), -0.2, 0.2), 2.0, 6.0)
    thickness = jnp.clip(jnp.exp(math.log(0.08) - 1.3862944 * jax.random.uniform(keys[5], (LEVELS,), jnp.float32) ** level_of(keys[5], (LEVELS,), ((0, 16),), -0.2, 0.2)), 0.02, 0.08)
    tracers = scatter_about(keys[6], (TRACERS, LEVELS, LATS, NLON), 1.0, 6.0, ((1, 16), (2, 64)), jnp.float32)
    return {"vort_div": vort_div, "legendre": legendre, "owner_map": owner_map, "lat_sine": lat_sine, "quad_weight": quad_weight, "thickness": thickness, "tracers": tracers}


planet_radius = 20.0

def spectral_winds(vort_div, wavenumbers, degrees):
    order = wavenumbers.astype(jnp.float32)[:, None]
    degree = jnp.arange(degrees).astype(jnp.float32)[None, :]
    ratio = jnp.maximum(degree * degree - order * order, 0.0) / jnp.maximum(4.0 * degree * degree - 1.0, 1.0)
    coupling = jnp.where(degree > order, jnp.sqrt(ratio), 0.0)
    inverse = jnp.where(degree > 0, -planet_radius * planet_radius / jnp.maximum(degree * (degree + 1.0), 1.0), 0.0)
    coupling_next = jnp.concatenate([coupling[:, 1:], jnp.zeros((coupling.shape[0], 1), jnp.float32)], axis=1)

    def derivative(field):
        edge = jnp.zeros(field.shape[:-1] + (1,), jnp.float32)
        lower = jnp.concatenate([edge, field[..., :-1]], axis=-1)
        upper = jnp.concatenate([field[..., 1:], edge], axis=-1)
        return -(degree - 1.0) * coupling * lower + (degree + 2.0) * coupling_next * upper
    stream_real = inverse * vort_div[0]
    stream_imag = inverse * vort_div[1]
    potential_real = inverse * vort_div[2]
    potential_imag = inverse * vort_div[3]
    east_real = (-order * potential_imag - derivative(stream_real)) / planet_radius
    east_imag = (order * potential_real - derivative(stream_imag)) / planet_radius
    north_real = (-order * stream_imag + derivative(potential_real)) / planet_radius
    north_imag = (order * stream_real + derivative(potential_imag)) / planet_radius
    return jnp.stack([east_real, east_imag, north_real, north_imag, vort_div[2], vort_div[3]], axis=0)

def reference(vort_div, legendre, owner_map, lat_sine, quad_weight, thickness, tracers):
    degrees = legendre.shape[2]
    order = owner_map.astype(jnp.float32)[:, None]
    degree = jnp.arange(degrees).astype(jnp.float32)[None, :]
    valid = degree >= order
    table = jnp.where(valid[:, None, :], legendre, 0.0)
    coefficients = spectral_winds(vort_div, owner_map, degrees)
    fourier = jnp.einsum('sjn,fksn->fkjs', table, coefficients, precision=lax.Precision.HIGHEST)
    real_part = fourier[0::2]
    imag_part = fourier[1::2]
    spread_real = jnp.zeros(real_part.shape, jnp.float32).at[..., owner_map].set(real_part)
    spread_imag = jnp.zeros(imag_part.shape, jnp.float32).at[..., owner_map].set(imag_part)
    first = jnp.arange(M) == 0
    half_real = jnp.where(first, spread_real, 0.5 * spread_real)
    half_imag = jnp.where(first, 0.0, 0.5 * spread_imag)
    spectrum = lax.complex(half_real, half_imag)
    spectrum = jnp.concatenate([spectrum, jnp.zeros(spectrum.shape[:-1] + (1,), spectrum.dtype)], axis=-1)
    grid_fields = NLON * jnp.fft.irfft(spectrum, n=NLON, axis=-1)
    east = grid_fields[0]
    north = grid_fields[1]
    divergence = grid_fields[2]
    layer_mass = divergence * thickness[:, None, None]
    column = jnp.cumsum(layer_mass, axis=0)
    omega_bottom = -column
    omega_top = layer_mass - column
    zero_level = jnp.zeros(tracers[:, :1].shape, jnp.float32)
    above = jnp.concatenate([zero_level, tracers[:, :-1]], axis=1)
    below = jnp.concatenate([tracers[:, 1:], zero_level], axis=1)
    vertical = (omega_bottom * (tracers + below) * 0.5 - omega_top * (above + tracers) * 0.5) / thickness[:, None, None]
    lon_step = 2.0 * math.pi / NLON
    lat_step = math.pi / M
    zonal_flux = east * tracers
    zonal = (jnp.roll(zonal_flux, -1, axis=3) - jnp.roll(zonal_flux, 1, axis=3)) / (2.0 * lon_step)
    merid_flux = north * tracers
    zero_row = jnp.zeros(merid_flux[:, :, :1].shape, jnp.float32)
    north_row = jnp.concatenate([merid_flux[:, :, 1:], zero_row], axis=2)
    south_row = jnp.concatenate([zero_row, merid_flux[:, :, :-1]], axis=2)
    merid = (north_row - south_row) / (2.0 * lat_step)
    metric = (1.0 - lat_sine * lat_sine)[None, None, :, None]
    grid_tendency = -quad_weight[None, None, :, None] * ((zonal + merid) / metric + vertical)
    transform = jnp.fft.rfft(grid_tendency, axis=-1)[..., :M]
    scale = 2.0 / NLON
    cos_part = scale * jnp.real(transform)
    sin_part = scale * jnp.imag(transform)
    stacked = jnp.stack([cos_part[..., owner_map], sin_part[..., owner_map]], axis=1)
    return jnp.einsum('sjn,crkjs->crksn', table, stacked, precision=lax.Precision.HIGHEST)
```

```python
import math

import jax
import jax.numpy as jnp
from jax import lax
from jax.experimental import pallas as pl
from jax.experimental.pallas import tpu as pltpu
from jax.sharding import PartitionSpec as P

planet_radius = 20.0
INTERPRET = False
f32 = jnp.float32
bf16 = jnp.bfloat16

vmem = pl.BlockSpec(memory_space=pltpu.VMEM)
smem = pl.BlockSpec(memory_space=pltpu.SMEM)


def halves(x):
    high = x.astype(bf16)
    low = (x - high.astype(f32)).astype(bf16)
    return high, low


def dot_nn(left, right):
    return lax.dot_general(left, right, (((1,), (0,)), ((), ())), preferred_element_type=f32)


def dot_nt(left, right):
    return lax.dot_general(left, right, (((1,), (1,)), ((), ())), preferred_element_type=f32)


def three_products(left, right_high, right_low, dot):
    rows = left.shape[0]
    high, low = halves(left)
    both = dot(jnp.concatenate([high, low], axis=0), right_high)
    return both[:rows] + both[rows:] + dot(high, right_low)


def cos_sin(steps, quarter):
    turns = jnp.floor(steps * (1.0 / quarter) + 0.5)
    angle = (steps - turns * quarter) * (0.5 * math.pi / quarter)
    z = angle * angle
    sine = ((-1.9515295891e-4 * z + 8.3321608736e-3) * z - 1.6666654611e-1) * z * angle + angle
    cosine = (
        (2.443315711809948e-5 * z - 1.388731625493765e-3) * z + 4.166664568298827e-2
    ) * z * z - 0.5 * z + 1.0
    turn = turns.astype(jnp.int32)
    odd = (turn & 1) == 1
    first = jnp.where(odd, sine, cosine)
    second = jnp.where(odd, cosine, sine)
    return (
        jnp.where(((turn + 1) & 2) == 2, -first, first),
        jnp.where((turn & 2) == 2, -second, second),
    )


def winds_kernel(vort_ref, leg_ref, order_ref, thick_ref, f_ref, lev_ref, ft_ref, msg_ref):
    slots, rows, degrees = leg_ref.shape
    copies = lev_ref.shape[0] // slots
    tiles = degrees // 128
    order = order_ref[...].astype(f32)

    def vort(part):
        start = part * slots * tiles
        return jnp.concatenate(
            [vort_ref[pl.ds(start + tile, slots, stride=tiles), :] for tile in range(tiles)], axis=1
        )

    degree = lax.broadcasted_iota(jnp.int32, (slots, degrees), 1).astype(f32)

    def coupling_at(n):
        ratio = jnp.maximum(n * n - order * order, 0.0) / jnp.maximum(4.0 * n * n - 1.0, 1.0)
        return jnp.where(n > order, jnp.sqrt(ratio), 0.0)

    coupling = coupling_at(degree)
    last = degree == degrees - 1
    coupling_next = jnp.where(last, 0.0, coupling_at(degree + 1.0))
    lower_factor = -(degree - 1.0) * coupling
    upper_factor = (degree + 2.0) * coupling_next
    inverse = jnp.where(
        degree > 0, -planet_radius * planet_radius / jnp.maximum(degree * (degree + 1.0), 1.0), 0.0
    )
    valid = degree >= order

    def derivative(field):
        lower = jnp.where(degree == 0, 0.0, pltpu.roll(field, 1, 1))
        upper = jnp.where(last, 0.0, pltpu.roll(field, degrees - 1, 1))
        return lower_factor * lower + upper_factor * upper

    div_real = vort(2)
    div_imag = vort(3)
    stream_real = inverse * vort(0)
    stream_imag = inverse * vort(1)
    potential_real = inverse * div_real
    potential_imag = inverse * div_imag
    scale = 1.0 / planet_radius
    thickness = thick_ref[0]
    zeros = jnp.zeros((slots, degrees), f32)
    fields = [
        (-order * potential_imag - derivative(stream_real)) * scale,
        (-order * stream_imag + derivative(potential_real)) * scale,
        div_real * thickness,
        zeros,
        (order * potential_real - derivative(stream_imag)) * scale,
        (order * stream_real + derivative(potential_imag)) * scale,
        div_imag * thickness,
        zeros,
    ]
    fields = [jnp.where(valid, field, 0.0) for field in fields]
    total = jnp.zeros((rows, 128), f32)
    for s in range(slots):
        lane = (s % 2) * 64 + (s // 2) * 8
        block = jnp.concatenate([field[s : s + 1] for field in fields], axis=0)
        parts = [block]
        if lane > 0:
            parts.insert(0, jnp.zeros((lane, degrees), f32))
        if lane + 8 < 128:
            parts.append(jnp.zeros((128 - lane - 8, degrees), f32))
        block_high, block_low = halves(jnp.concatenate(parts, axis=0))
        total = total + three_products(leg_ref[s], block_high, block_low, dot_nt)
    f_ref[...] = total
    ft_ref[...] = total.T
    for s in range(slots):
        lane = (s % 2) * 64 + (s // 2) * 8
        msg_ref[s : s + 1, 0:rows] = ft_ref[lane + 2 : lane + 3, :]
        msg_ref[s : s + 1, rows : 2 * rows] = ft_ref[lane + 6 : lane + 7, :]
    message = msg_ref[...]
    for copy in range(copies):
        lev_ref[copy * slots : (copy + 1) * slots, :] = message


def table_kernel(owner_ref, table_high_ref, table_low_ref, phase_cos_ref, phase_sin_ref):
    waves, slots = owner_ref.shape
    length = 2.0 * waves * slots
    orders = owner_ref[...].astype(f32)
    offset = lax.broadcasted_iota(jnp.int32, (waves, 128), 1).astype(f32)
    padded = jnp.concatenate([orders, jnp.zeros((waves, 128 - slots), f32)], axis=1)
    by_slot = padded.T
    blocks = phase_cos_ref.shape[0] // (slots // 2)
    block = lax.broadcasted_iota(jnp.int32, (blocks, 128), 0).astype(f32)
    for s in range(slots):
        cosine, sine = cos_sin(orders[:, s : s + 1] * offset, length / 4.0)
        cos_high, cos_low = halves(cosine)
        sin_high, sin_low = halves(-sine)
        rows = slice(s * waves, (s + 1) * waves)
        table_high_ref[rows, 0:128] = cos_high
        table_high_ref[rows, 128:256] = sin_high
        table_low_ref[rows, 0:128] = cos_low
        table_low_ref[rows, 128:256] = sin_low
    for t in range(slots // 2):
        row = jnp.concatenate([by_slot[2 * t : 2 * t + 1, :], by_slot[2 * t + 1 : 2 * t + 2, :]], axis=1)
        cosine, sine = cos_sin(row * block * 128.0, length / 4.0)
        phase_cos_ref[t * blocks : (t + 1) * blocks, :] = cosine
        phase_sin_ref[t * blocks : (t + 1) * blocks, :] = sine


def prefix_kernel(got_ref, f_ref, level_ref, out_ref, ft_ref):
    rows = f_ref.shape[0]
    slots = 10
    copies = got_ref.shape[0] // slots
    level = level_ref[0]
    total = jnp.zeros((slots, 128), f32)
    for source in range(copies):
        total = total + jnp.where(source < level, got_ref[source * slots : (source + 1) * slots, :], 0.0)
    ft_ref[...] = jnp.zeros((128, rows), f32)
    for s in range(slots):
        lane = (s % 2) * 64 + (s // 2) * 8
        ft_ref[lane + 3 : lane + 4, :] = total[s : s + 1, 0:rows]
        ft_ref[lane + 7 : lane + 8, :] = total[s : s + 1, rows : 2 * rows]
    out_ref[...] = f_ref[...] + ft_ref[...].T


def grid_kernel(
    got_ref,
    table_high_ref,
    table_low_ref,
    phase_cos_ref,
    phase_sin_ref,
    q_ref,
    above_ref,
    below_ref,
    sine_ref,
    weight_ref,
    thick_ref,
    out_ref,
):
    waves = got_ref.shape[0]
    pairs = 5
    blocks = phase_cos_ref.shape[0] // pairs
    used = q_ref.shape[0] // 8
    got = got_ref[...]
    stacked = jnp.concatenate([got, pltpu.roll(got, 64, 1)], axis=0).T
    sign = jnp.where(lax.broadcasted_iota(jnp.int32, (8, 128), 0) < 4, -1.0, 1.0)
    plain = [stacked[8 * t : 8 * t + 8] for t in range(pairs)]
    swapped = [pltpu.roll(x, 4, 0) * sign for x in plain]
    phase_cos = [[phase_cos_ref[t * blocks + b : t * blocks + b + 1, :] for t in range(pairs)] for b in range(used)]
    phase_sin = [[phase_sin_ref[t * blocks + b : t * blocks + b + 1, :] for t in range(pairs)] for b in range(used)]
    turned = jnp.concatenate(
        [
            jnp.concatenate(
                [plain[t] * phase_cos[b][t] + swapped[t] * phase_sin[b][t] for t in range(pairs)], axis=1
            )
            for b in range(used)
        ],
        axis=0,
    )
    table_high = table_high_ref[...]
    table_low = table_low_ref[...]
    grid = three_products(turned, table_high, table_low, dot_nn)
    length = 128.0 * used
    lon_step = 2.0 * math.pi / length
    lat_step = 2.0 * math.pi / length
    sine = sine_ref[0]
    metric = 1.0 - sine * sine
    weight = -weight_ref[0] * (2.0 / length)
    zonal_factor = weight / (metric * (2.0 * lon_step))
    merid_factor = weight / (metric * (2.0 * lat_step))
    vertical_factor = weight / (2.0 * thick_ref[0])
    lane = lax.broadcasted_iota(jnp.int32, (8, 128), 1)
    tracer, east, other, merid = [], [], [], []
    for b in range(used):
        q = q_ref[pl.ds(b, 8, stride=used), :]
        above = above_ref[pl.ds(b, 8, stride=used), :]
        below = below_ref[pl.ds(b, 8, stride=used), :]
        field = grid[8 * b : 8 * b + 4, 0:128] + grid[8 * b + 4 : 8 * b + 8, 128:256]
        east.append(field[0:1] * q)
        merid.append(field[1:2] * q)
        other.append((field[3:4] * (above - below) - field[2:3] * (q + below)) * vertical_factor)
    ahead = [pltpu.roll(z, 127, 1) for z in east]
    behind = [pltpu.roll(z, 1, 1) for z in east]
    rest = []
    for b in range(used):
        right = jnp.where(lane == 127, ahead[(b + 1) % used], ahead[b])
        left = jnp.where(lane == 0, behind[(b - 1) % used], behind[b])
        rest.append(other[b] + zonal_factor * (right - left))
    values = jnp.concatenate(rest + merid, axis=0)
    along_cos = three_products(values, table_high[:, 0:128], table_low[:, 0:128], dot_nt)
    along_sin = three_products(values, table_high[:, 128:256], table_low[:, 128:256], dot_nt)
    for kind in range(2):
        stack = []
        for t in range(pairs):
            cos_total = jnp.zeros((8, 128), f32)
            sin_total = jnp.zeros((8, 128), f32)
            for b in range(used):
                row = 8 * (kind * used + b)
                c = along_cos[row : row + 8, 128 * t : 128 * t + 128]
                s = along_sin[row : row + 8, 128 * t : 128 * t + 128]
                cos_total = cos_total + phase_cos[b][t] * c + phase_sin[b][t] * s
                sin_total = sin_total + phase_cos[b][t] * s - phase_sin[b][t] * c
            stack += [cos_total, sin_total]
        stack.append(jnp.full((128 - 16 * pairs, 128), merid_factor, f32))
        sent = jnp.concatenate(stack, axis=0).T
        for parity in range(2):
            out_ref[pl.ds(kind * 2 + parity, waves, stride=4), :] = sent[parity * 64 : parity * 64 + waves]


def result_kernel(got_ref, leg_ref, order_ref, out_ref):
    slots, rows, degrees = leg_ref.shape
    tiles = degrees // 128
    zero_row = jnp.zeros((1, 128), f32)
    parts = []
    for parity in range(2):
        rest = got_ref[pl.ds(parity, rows, stride=4), :]
        merid = got_ref[pl.ds(2 + parity, rows, stride=4), :]
        factor = rest[:, 80:81]
        north = jnp.concatenate([merid[1:], zero_row], axis=0)
        south = jnp.concatenate([zero_row, merid[:-1]], axis=0)
        parts.append(rest + factor * (north - south))
    stacked = jnp.concatenate(parts, axis=0).T
    first = lax.broadcasted_iota(jnp.int32, (16, 2 * rows), 1) < rows
    degree = lax.broadcasted_iota(jnp.int32, (8, degrees), 1)
    for t in range(slots // 2):
        block = stacked[16 * t : 16 * t + 16]
        left = jnp.concatenate([jnp.where(first, block, 0.0), jnp.where(first, 0.0, block)], axis=0)
        right = leg_ref[2 * t : 2 * t + 2].reshape(2 * rows, degrees)
        right_high, right_low = halves(right)
        product = three_products(left, right_high, right_low, dot_nn)
        for parity in range(2):
            s = 2 * t + parity
            valid = degree >= order_ref[s]
            for part in range(2):
                row = parity * 16 + part * 8
                kept = jnp.where(valid, product[row : row + 8], 0.0)
                for tile in range(tiles):
                    start = (part * slots + s) * tiles + tile
                    out_ref[pl.ds(start, 8, stride=2 * slots * tiles), :] = kept[:, 128 * tile : 128 * tile + 128]


def local(x):
    return x if INTERPRET else pltpu.with_memory_space_constraint(x, pltpu.VMEM)


def shaped(shape, dtype=f32):
    return jax.ShapeDtypeStruct(shape, dtype) if INTERPRET else pltpu.VMEM(shape, dtype)


def shards(vort_div, legendre, owner_map, lat_sine, quad_weight, thickness, tracers):
    slots, rows, degrees = legendre.shape
    waves = lax.axis_size("wave")
    levels = lax.axis_size("lev")
    count, _, _, length = tracers.shape
    call = lambda kernel, **kw: pl.pallas_call(kernel, interpret=INTERPRET, **kw)
    up = [(i, i + 1) for i in range(levels - 1)]
    down = [(b, a) for a, b in up]
    above = lax.ppermute(tracers, "lev", up)
    below = lax.ppermute(tracers, "lev", down)
    legendre = local(legendre)
    own = lax.dynamic_slice_in_dim(owner_map, lax.axis_index("wave") * slots, slots)
    level = lax.axis_index("lev").astype(jnp.int32).reshape(1)
    fourier, message = call(
        winds_kernel,
        name="winds",
        in_specs=[vmem, vmem, vmem, smem],
        out_specs=(vmem, vmem),
        out_shape=(
            shaped((rows, 128)),
            shaped((levels * slots, 128)),
        ),
        scratch_shapes=[pltpu.VMEM((128, rows), f32), pltpu.VMEM((slots, 128), f32)],
    )(local(vort_div.reshape(4 * slots * degrees // 128, 128)), legendre, local(own.reshape(slots, 1)), thickness)
    totals = lax.all_to_all(
        message.reshape(levels, 1, slots * 128), "lev", split_axis=0, concat_axis=0, tiled=True
    ).reshape(levels * slots, 128)
    table_high, table_low, phase_cos, phase_sin = call(
        table_kernel,
        name="tables",
        in_specs=[vmem],
        out_specs=(vmem, vmem, vmem, vmem),
        out_shape=(
            shaped((waves * slots, 256), bf16),
            shaped((waves * slots, 256), bf16),
            shaped((slots // 2 * 16, 128)),
            shaped((slots // 2 * 16, 128)),
        ),
    )(local(owner_map.reshape(waves, slots)))
    sent = call(
        prefix_kernel,
        name="prefix",
        in_specs=[vmem, vmem, smem],
        out_specs=vmem,
        out_shape=shaped((rows, 128)),
        scratch_shapes=[pltpu.VMEM((128, rows), f32)],
    )(local(totals), local(fourier), level)
    got = lax.all_to_all(
        sent.reshape(rows, 1, 128), "wave", split_axis=0, concat_axis=0, tiled=True
    ).reshape(waves, 128)
    flat = lambda x: local(x.reshape(count * length // 128, 128))
    spectra = call(
        grid_kernel,
        name="grid",
        in_specs=[vmem] * 8 + [smem] * 3,
        out_specs=vmem,
        out_shape=shaped((waves * 4, 128)),
    )(
        local(got),
        local(table_high),
        local(table_low),
        local(phase_cos),
        local(phase_sin),
        flat(tracers),
        flat(above),
        flat(below),
        lat_sine,
        quad_weight,
        thickness,
    )
    back = lax.all_to_all(
        spectra.reshape(waves, 4, 128), "wave", split_axis=0, concat_axis=0, tiled=True
    ).reshape(rows * 4, 128)
    result = call(
        result_kernel,
        name="result",
        in_specs=[vmem, vmem, smem],
        out_specs=vmem,
        out_shape=jax.ShapeDtypeStruct((count * 2 * slots * degrees // 128, 128), f32),
    )(local(back), legendre, own)
    return result.reshape(count, 2, 1, slots, degrees)


def solution(mesh):
    placed = (
        P(None, "lev", "wave", None),
        P("wave", None, None),
        P(),
        P("wave"),
        P("wave"),
        P("lev"),
        P(None, "lev", "wave", None),
    )
    return jax.shard_map(
        shards,
        mesh=mesh,
        in_specs=placed,
        out_specs=P(None, None, "lev", "wave", None),
        check_vma=False,
    )
```

```python
import math

import jax
import jax.numpy as jnp
from jax import lax
from jax.experimental import pallas as pl
from jax.experimental.pallas import tpu as pltpu
from jax.sharding import PartitionSpec as P


planet_radius = 20.0
INTERPRET = False
f32 = jnp.float32
bf16 = jnp.bfloat16

vmem = pl.BlockSpec(memory_space=pltpu.VMEM)
hbm = pl.BlockSpec(memory_space=pl.ANY)
smem = pl.BlockSpec(memory_space=pltpu.SMEM)


def halves(x):
    high = x.astype(bf16)
    low = (x - high.astype(f32)).astype(bf16)
    return high, low


def dot_nn(left, right):
    return lax.dot_general(left, right, (((1,), (0,)), ((), ())), preferred_element_type=f32)


def dot_nt(left, right):
    return lax.dot_general(left, right, (((1,), (1,)), ((), ())), preferred_element_type=f32)


def three_products(left, right_high, right_low, dot):
    rows = left.shape[0]
    high, low = halves(left)
    both = dot(jnp.concatenate([high, low], axis=0), right_high)
    return both[:rows] + both[rows:] + dot(high, right_low)


def cos_sin(steps, quarter):
    turns = jnp.floor(steps * (1.0 / quarter) + 0.5)
    angle = (steps - turns * quarter) * (0.5 * math.pi / quarter)
    z = angle * angle
    sine = ((-1.9515295891e-4 * z + 8.3321608736e-3) * z - 1.6666654611e-1) * z * angle + angle
    cosine = (
        (2.443315711809948e-5 * z - 1.388731625493765e-3) * z + 4.166664568298827e-2
    ) * z * z - 0.5 * z + 1.0
    turn = turns.astype(jnp.int32)
    odd = (turn & 1) == 1
    first = jnp.where(odd, sine, cosine)
    second = jnp.where(odd, cosine, sine)
    return (
        jnp.where(((turn + 1) & 2) == 2, -first, first),
        jnp.where((turn & 2) == 2, -second, second),
    )


def own_orders(owner_ref, slots):
    start = lax.axis_index("wave") * slots if not INTERPRET else owner_ref[owner_ref.shape[0] - 1] * slots
    return [owner_ref[start + s] for s in range(slots)]


def winds_kernel(
    vort_hbm,
    leg_hbm,
    owner_hbm,
    thick_ref,
    f_ref,
    lev_ref,
    high_ref,
    low_ref,
    vort_ref,
    leg_ref,
    owner_ref,
    ft_ref,
    msg_ref,
    sem,
    leg_sem,
):
    slots, rows, degrees = leg_ref.shape
    copies = lev_ref.shape[0] // slots
    tiles = degrees // 128
    vort_copy = pltpu.make_async_copy(vort_hbm, vort_ref, sem.at[0])
    owner_copy = pltpu.make_async_copy(owner_hbm, owner_ref, sem.at[1])
    owner_copy.start()
    vort_copy.start()
    leg_copies = []
    for s in range(slots):
        leg_copies.append(pltpu.make_async_copy(leg_hbm.at[s], leg_ref.at[s], leg_sem.at[s]))
        leg_copies[s].start()
    owner_copy.wait()
    own = own_orders(owner_ref, slots)
    row = lax.broadcasted_iota(jnp.int32, (slots, degrees), 0)
    order = jnp.zeros((slots, degrees), f32)
    for s in range(slots):
        order = jnp.where(row == s, own[s].astype(f32), order)

    def vort(part):
        start = part * slots * tiles
        return jnp.concatenate(
            [vort_ref[pl.ds(start + tile, slots, stride=tiles), :] for tile in range(tiles)], axis=1
        )

    degree = lax.broadcasted_iota(jnp.int32, (slots, degrees), 1).astype(f32)

    def coupling_at(n):
        ratio = jnp.maximum(n * n - order * order, 0.0) / jnp.maximum(4.0 * n * n - 1.0, 1.0)
        return jnp.where(n > order, jnp.sqrt(ratio), 0.0)

    coupling = coupling_at(degree)
    last = degree == degrees - 1
    coupling_next = jnp.where(last, 0.0, coupling_at(degree + 1.0))
    lower_factor = -(degree - 1.0) * coupling
    upper_factor = (degree + 2.0) * coupling_next
    inverse = jnp.where(
        degree > 0, -planet_radius * planet_radius / jnp.maximum(degree * (degree + 1.0), 1.0), 0.0
    )
    valid = degree >= order

    def derivative(field):
        lower = jnp.where(degree == 0, 0.0, pltpu.roll(field, 1, 1))
        upper = jnp.where(last, 0.0, pltpu.roll(field, degrees - 1, 1))
        return lower_factor * lower + upper_factor * upper

    vort_copy.wait()
    div_real = vort(2)
    div_imag = vort(3)
    stream_real = inverse * vort(0)
    stream_imag = inverse * vort(1)
    potential_real = inverse * div_real
    potential_imag = inverse * div_imag
    scale = 1.0 / planet_radius
    thickness = thick_ref[0]
    zeros = jnp.zeros((slots, degrees), f32)
    fields = [
        (-order * potential_imag - derivative(stream_real)) * scale,
        (-order * stream_imag + derivative(potential_real)) * scale,
        div_real * thickness,
        zeros,
        (order * potential_real - derivative(stream_imag)) * scale,
        (order * stream_real + derivative(potential_imag)) * scale,
        div_imag * thickness,
        zeros,
    ]
    fields = [jnp.where(valid, field, 0.0) for field in fields]
    total = jnp.zeros((rows, 128), f32)
    for s in range(slots):
        lane = (s % 2) * 64 + (s // 2) * 8
        block = jnp.concatenate([field[s : s + 1] for field in fields], axis=0)
        parts = [block]
        if lane > 0:
            parts.insert(0, jnp.zeros((lane, degrees), f32))
        if lane + 8 < 128:
            parts.append(jnp.zeros((128 - lane - 8, degrees), f32))
        block_high, block_low = halves(jnp.concatenate(parts, axis=0))
        leg_copies[s].wait()
        leg_high, leg_low = halves(leg_ref[s])
        high_ref[s * rows : (s + 1) * rows, :] = leg_high
        low_ref[s * rows : (s + 1) * rows, :] = leg_low
        both = dot_nt(jnp.concatenate([leg_high, leg_low], axis=0), block_high)
        total = total + (both[:rows] + both[rows:] + dot_nt(leg_high, block_low))
    f_ref[...] = total
    ft_ref[...] = total.T
    for s in range(slots):
        lane = (s % 2) * 64 + (s // 2) * 8
        msg_ref[s : s + 1, 0:rows] = ft_ref[lane + 2 : lane + 3, :]
        msg_ref[s : s + 1, rows : 2 * rows] = ft_ref[lane + 6 : lane + 7, :]
    message = msg_ref[...]
    for copy in range(copies):
        lev_ref[copy * slots : (copy + 1) * slots, :] = message


def table_kernel(owner_ref, table_high_ref, table_low_ref, phase_cos_ref, phase_sin_ref):
    waves, slots = owner_ref.shape
    length = 2.0 * waves * slots
    orders = owner_ref[...].astype(f32)
    offset = lax.broadcasted_iota(jnp.int32, (waves, 128), 1).astype(f32)
    padded = jnp.concatenate([orders, jnp.zeros((waves, 128 - slots), f32)], axis=1)
    by_slot = padded.T
    blocks = phase_cos_ref.shape[0] // (slots // 2)
    block = lax.broadcasted_iota(jnp.int32, (blocks, 128), 0).astype(f32)
    for s in range(slots):
        cosine, sine = cos_sin(orders[:, s : s + 1] * offset, length / 4.0)
        cos_high, cos_low = halves(cosine)
        sin_high, sin_low = halves(-sine)
        rows = slice(s * waves, (s + 1) * waves)
        table_high_ref[rows, 0:128] = cos_high
        table_high_ref[rows, 128:256] = sin_high
        table_low_ref[rows, 0:128] = cos_low
        table_low_ref[rows, 128:256] = sin_low
    for t in range(slots // 2):
        row = jnp.concatenate([by_slot[2 * t : 2 * t + 1, :], by_slot[2 * t + 1 : 2 * t + 2, :]], axis=1)
        cosine, sine = cos_sin(row * block * 128.0, length / 4.0)
        phase_cos_ref[t * blocks : (t + 1) * blocks, :] = cosine
        phase_sin_ref[t * blocks : (t + 1) * blocks, :] = sine


def prefix_kernel(got_ref, f_ref, level_ref, out_ref, ft_ref):
    rows = f_ref.shape[0]
    slots = 10
    copies = got_ref.shape[0] // slots
    level = level_ref[0]
    total = jnp.zeros((slots, 128), f32)
    for source in range(copies):
        total = total + jnp.where(source < level, got_ref[source * slots : (source + 1) * slots, :], 0.0)
    ft_ref[...] = jnp.zeros((128, rows), f32)
    for s in range(slots):
        lane = (s % 2) * 64 + (s // 2) * 8
        ft_ref[lane + 3 : lane + 4, :] = total[s : s + 1, 0:rows]
        ft_ref[lane + 7 : lane + 8, :] = total[s : s + 1, rows : 2 * rows]
    out_ref[...] = f_ref[...] + ft_ref[...].T


def grid_kernel(
    got_ref,
    table_high_ref,
    table_low_ref,
    phase_cos_ref,
    phase_sin_ref,
    q_ref,
    above_ref,
    below_ref,
    sine_ref,
    weight_ref,
    thick_ref,
    out_ref,
):
    waves = got_ref.shape[0]
    pairs = 5
    blocks = phase_cos_ref.shape[0] // pairs
    used = q_ref.shape[0] // 8
    got = got_ref[...]
    stacked = jnp.concatenate([got, pltpu.roll(got, 64, 1)], axis=0).T
    sign = jnp.where(lax.broadcasted_iota(jnp.int32, (8, 128), 0) < 4, -1.0, 1.0)
    plain = [stacked[8 * t : 8 * t + 8] for t in range(pairs)]
    swapped = [pltpu.roll(x, 4, 0) * sign for x in plain]
    phase_cos = [[phase_cos_ref[t * blocks + b : t * blocks + b + 1, :] for t in range(pairs)] for b in range(used)]
    phase_sin = [[phase_sin_ref[t * blocks + b : t * blocks + b + 1, :] for t in range(pairs)] for b in range(used)]
    turned = jnp.concatenate(
        [
            jnp.concatenate(
                [plain[t] * phase_cos[b][t] + swapped[t] * phase_sin[b][t] for t in range(pairs)], axis=1
            )
            for b in range(used)
        ],
        axis=0,
    )
    table_high = table_high_ref[...]
    table_low = table_low_ref[...]
    grid = three_products(turned, table_high, table_low, dot_nn)
    length = 128.0 * used
    lon_step = 2.0 * math.pi / length
    lat_step = 2.0 * math.pi / length
    sine = sine_ref[0]
    metric = 1.0 - sine * sine
    weight = -weight_ref[0] * (2.0 / length)
    zonal_factor = weight / (metric * (2.0 * lon_step))
    merid_factor = weight / (metric * (2.0 * lat_step))
    vertical_factor = weight / (2.0 * thick_ref[0])
    lane = lax.broadcasted_iota(jnp.int32, (8, 128), 1)
    east, other, merid = [], [], []
    for b in range(used):
        q = q_ref[pl.ds(b, 8, stride=used), :]
        above = above_ref[pl.ds(b, 8, stride=used), :]
        below = below_ref[pl.ds(b, 8, stride=used), :]
        field = grid[8 * b : 8 * b + 4, 0:128] + grid[8 * b + 4 : 8 * b + 8, 128:256]
        east.append(field[0:1] * q)
        merid.append(field[1:2] * q)
        other.append((field[3:4] * (above - below) - field[2:3] * (q + below)) * vertical_factor)
    ahead = [pltpu.roll(z, 127, 1) for z in east]
    behind = [pltpu.roll(z, 1, 1) for z in east]
    rest = []
    for b in range(used):
        right = jnp.where(lane == 127, ahead[(b + 1) % used], ahead[b])
        left = jnp.where(lane == 0, behind[(b - 1) % used], behind[b])
        rest.append(other[b] + zonal_factor * (right - left))
    values = jnp.concatenate(rest + merid, axis=0)
    along_cos = three_products(values, table_high[:, 0:128], table_low[:, 0:128], dot_nt)
    along_sin = three_products(values, table_high[:, 128:256], table_low[:, 128:256], dot_nt)
    for kind in range(2):
        stack = []
        for t in range(pairs):
            cos_total = jnp.zeros((8, 128), f32)
            sin_total = jnp.zeros((8, 128), f32)
            for b in range(used):
                row = 8 * (kind * used + b)
                c = along_cos[row : row + 8, 128 * t : 128 * t + 128]
                s = along_sin[row : row + 8, 128 * t : 128 * t + 128]
                cos_total = cos_total + phase_cos[b][t] * c + phase_sin[b][t] * s
                sin_total = sin_total + phase_cos[b][t] * s - phase_sin[b][t] * c
            stack += [cos_total, sin_total]
        stack.append(jnp.full((128 - 16 * pairs, 128), merid_factor, f32))
        sent = jnp.concatenate(stack, axis=0).T
        for parity in range(2):
            out_ref[pl.ds(kind * 2 + parity, waves, stride=4), :] = sent[parity * 64 : parity * 64 + waves]


def result_kernel(got_ref, high_ref, low_ref, owner_ref, out_ref):
    degrees = high_ref.shape[1]
    rows = got_ref.shape[0] // 4
    slots = high_ref.shape[0] // rows
    tiles = degrees // 128
    own = own_orders(owner_ref, slots)
    zero_row = jnp.zeros((1, 128), f32)
    parts = []
    for parity in range(2):
        rest = got_ref[pl.ds(parity, rows, stride=4), :]
        merid = got_ref[pl.ds(2 + parity, rows, stride=4), :]
        factor = rest[:, 80:81]
        north = jnp.concatenate([merid[1:], zero_row], axis=0)
        south = jnp.concatenate([zero_row, merid[:-1]], axis=0)
        parts.append(rest + factor * (north - south))
    stacked = jnp.concatenate(parts, axis=0).T
    first = lax.broadcasted_iota(jnp.int32, (16, 2 * rows), 1) < rows
    degree = lax.broadcasted_iota(jnp.int32, (8, degrees), 1)
    for t in range(slots // 2):
        block = stacked[16 * t : 16 * t + 16]
        left = jnp.concatenate([jnp.where(first, block, 0.0), jnp.where(first, 0.0, block)], axis=0)
        pair = slice(2 * t * rows, 2 * (t + 1) * rows)
        product = three_products(left, high_ref[pair, :], low_ref[pair, :], dot_nn)
        for parity in range(2):
            s = 2 * t + parity
            valid = degree >= own[s]
            for part in range(2):
                row = parity * 16 + part * 8
                kept = jnp.where(valid, product[row : row + 8], 0.0)
                for tile in range(tiles):
                    start = (part * slots + s) * tiles + tile
                    out_ref[pl.ds(start, 8, stride=2 * slots * tiles), :] = kept[:, 128 * tile : 128 * tile + 128]


def local(x):
    return x if INTERPRET else pltpu.with_memory_space_constraint(x, pltpu.VMEM)


def shaped(shape, dtype=f32):
    return jax.ShapeDtypeStruct(shape, dtype) if INTERPRET else pltpu.VMEM(shape, dtype)


def shards(vort_div, legendre, owner_map, lat_sine, quad_weight, thickness, tracers):
    slots, rows, degrees = legendre.shape
    waves = lax.axis_size("wave")
    levels = lax.axis_size("lev")
    count, _, _, length = tracers.shape
    call = lambda kernel, **kw: pl.pallas_call(kernel, interpret=INTERPRET, **kw)
    up = [(i, i + 1) for i in range(levels - 1)]
    down = [(b, a) for a, b in up]
    above = lax.ppermute(tracers, "lev", up)
    below = lax.ppermute(tracers, "lev", down)
    owner = owner_map
    if INTERPRET:
        owner = jnp.concatenate([owner_map, lax.axis_index("wave").reshape(1)])
    level = lax.axis_index("lev").astype(jnp.int32).reshape(1)
    fourier, message, leg_high, leg_low = call(
        winds_kernel,
        name="winds",
        in_specs=[hbm, hbm, hbm, smem],
        out_specs=(vmem, vmem, vmem, vmem),
        out_shape=(
            shaped((rows, 128)),
            shaped((levels * slots, 128)),
            shaped((slots * rows, degrees), bf16),
            shaped((slots * rows, degrees), bf16),
        ),
        scratch_shapes=[
            pltpu.VMEM((4 * slots * degrees // 128, 128), f32),
            pltpu.VMEM((slots, rows, degrees), f32),
            pltpu.SMEM(owner.shape, jnp.int32),
            pltpu.VMEM((128, rows), f32),
            pltpu.VMEM((slots, 128), f32),
            pltpu.SemaphoreType.DMA((2,)),
            pltpu.SemaphoreType.DMA((slots,)),
        ],
    )(vort_div.reshape(4 * slots * degrees // 128, 128), legendre, owner, thickness)
    totals = lax.all_to_all(
        message.reshape(levels, 1, slots * 128), "lev", split_axis=0, concat_axis=0, tiled=True
    ).reshape(levels * slots, 128)
    table_high, table_low, phase_cos, phase_sin = call(
        table_kernel,
        name="tables",
        in_specs=[vmem],
        out_specs=(vmem, vmem, vmem, vmem),
        out_shape=(
            shaped((waves * slots, 256), bf16),
            shaped((waves * slots, 256), bf16),
            shaped((slots // 2 * 16, 128)),
            shaped((slots // 2 * 16, 128)),
        ),
    )(local(owner_map.reshape(waves, slots)))
    sent = call(
        prefix_kernel,
        name="prefix",
        in_specs=[vmem, vmem, smem],
        out_specs=vmem,
        out_shape=shaped((rows, 128)),
        scratch_shapes=[pltpu.VMEM((128, rows), f32)],
    )(local(totals), local(fourier), level)
    got = lax.all_to_all(
        sent.reshape(rows, 1, 128), "wave", split_axis=0, concat_axis=0, tiled=True
    ).reshape(waves, 128)
    flat = lambda x: local(x.reshape(count * length // 128, 128))
    spectra = call(
        grid_kernel,
        name="grid",
        in_specs=[vmem] * 8 + [smem] * 3,
        out_specs=vmem,
        out_shape=shaped((waves * 4, 128)),
    )(
        local(got),
        local(table_high),
        local(table_low),
        local(phase_cos),
        local(phase_sin),
        flat(tracers),
        flat(above),
        flat(below),
        lat_sine,
        quad_weight,
        thickness,
    )
    back = lax.all_to_all(
        spectra.reshape(waves, 4, 128), "wave", split_axis=0, concat_axis=0, tiled=True
    ).reshape(rows * 4, 128)
    result = call(
        result_kernel,
        name="result",
        in_specs=[vmem, vmem, vmem, smem],
        out_specs=vmem,
        out_shape=jax.ShapeDtypeStruct((count * 2 * slots * degrees // 128, 128), f32),
    )(local(back), local(leg_high), local(leg_low), owner)
    return result.reshape(count, 2, 1, slots, degrees)


def solution(mesh):
    placed = (
        P(None, "lev", "wave", None),
        P("wave", None, None),
        P(),
        P("wave"),
        P("wave"),
        P("lev"),
        P(None, "lev", "wave", None),
    )

    return jax.shard_map(
        shards,
        mesh=mesh,
        in_specs=placed,
        out_specs=P(None, None, "lev", "wave", None),
        check_vma=False,
    )
```

```python
import math

import jax
import jax.numpy as jnp
from jax import lax
from jax.experimental import pallas as pl
from jax.experimental.pallas import tpu as pltpu
from jax.sharding import PartitionSpec as P


planet_radius = 20.0
INTERPRET = False
f32 = jnp.float32
bf16 = jnp.bfloat16

vmem = pl.BlockSpec(memory_space=pltpu.VMEM)
hbm = pl.BlockSpec(memory_space=pltpu.HBM)
smem = pl.BlockSpec(memory_space=pltpu.SMEM)


def halves(x):
    high = x.astype(bf16)
    low = (x - high.astype(f32)).astype(bf16)
    return high, low


def dot_nn(left, right):
    return lax.dot_general(left, right, (((1,), (0,)), ((), ())), preferred_element_type=f32)


def dot_nt(left, right):
    return lax.dot_general(left, right, (((1,), (1,)), ((), ())), preferred_element_type=f32)


def three_products(left, right_high, right_low, dot):
    rows = left.shape[0]
    high, low = halves(left)
    both = dot(jnp.concatenate([high, low], axis=0), right_high)
    return both[:rows] + both[rows:] + dot(high, right_low)


def cos_sin(steps, quarter):
    turns = jnp.floor(steps * (1.0 / quarter) + 0.5)
    angle = (steps - turns * quarter) * (0.5 * math.pi / quarter)
    z = angle * angle
    sine = ((-1.9515295891e-4 * z + 8.3321608736e-3) * z - 1.6666654611e-1) * z * angle + angle
    cosine = (
        (2.443315711809948e-5 * z - 1.388731625493765e-3) * z + 4.166664568298827e-2
    ) * z * z - 0.5 * z + 1.0
    turn = turns.astype(jnp.int32)
    odd = (turn & 1) == 1
    first = jnp.where(odd, sine, cosine)
    second = jnp.where(odd, cosine, sine)
    return (
        jnp.where(((turn + 1) & 2) == 2, -first, first),
        jnp.where((turn & 2) == 2, -second, second),
    )


def own_orders(owner_ref, slots):
    start = lax.axis_index("wave") * slots if not INTERPRET else owner_ref[owner_ref.shape[0] - 1] * slots
    return [owner_ref[start + s] for s in range(slots)]


def winds_kernel(
    vort_hbm,
    leg_hbm,
    owner_hbm,
    thick_hbm,
    f_ref,
    lev_ref,
    high_ref,
    low_ref,
    vort_ref,
    leg_ref,
    owner_ref,
    thick_ref,
    field_ref,
    msg_ref,
    sem,
    leg_sem,
):
    slots, rows, degrees = leg_ref.shape
    copies = lev_ref.shape[0] // slots
    tiles = degrees // 128
    vort_copy = pltpu.make_async_copy(vort_hbm, vort_ref, sem.at[0])
    owner_copy = pltpu.make_async_copy(owner_hbm, owner_ref, sem.at[1])
    thick_copy = pltpu.make_async_copy(thick_hbm, thick_ref, sem.at[2])
    owner_copy.start(priority=1)
    thick_copy.start(priority=1)
    vort_copy.start(priority=1)

    def leg_copy(s):
        return pltpu.make_async_copy(leg_hbm.at[s], leg_ref.at[s], leg_sem.at[s])

    lax.fori_loop(0, slots, lambda s, _: leg_copy(s).start(), None)
    owner_copy.wait()
    own = own_orders(owner_ref, slots)
    row = lax.broadcasted_iota(jnp.int32, (slots, degrees), 0)
    order = jnp.zeros((slots, degrees), f32)
    for s in range(slots):
        order = jnp.where(row == s, own[s].astype(f32), order)

    def vort(part):
        start = part * slots * tiles
        return jnp.concatenate(
            [vort_ref[pl.ds(start + tile, slots, stride=tiles), :] for tile in range(tiles)], axis=1
        )

    degree = lax.broadcasted_iota(jnp.int32, (slots, degrees), 1).astype(f32)

    def coupling_at(n):
        ratio = jnp.maximum(n * n - order * order, 0.0) / jnp.maximum(4.0 * n * n - 1.0, 1.0)
        return jnp.where(n > order, jnp.sqrt(ratio), 0.0)

    coupling = coupling_at(degree)
    last = degree == degrees - 1
    coupling_next = jnp.where(last, 0.0, coupling_at(degree + 1.0))
    lower_factor = -(degree - 1.0) * coupling
    upper_factor = (degree + 2.0) * coupling_next
    inverse = jnp.where(
        degree > 0, -planet_radius * planet_radius / jnp.maximum(degree * (degree + 1.0), 1.0), 0.0
    )
    valid = degree >= order

    def derivative(field):
        lower = jnp.where(degree == 0, 0.0, pltpu.roll(field, 1, 1))
        upper = jnp.where(last, 0.0, pltpu.roll(field, degrees - 1, 1))
        return lower_factor * lower + upper_factor * upper

    vort_copy.wait()
    thick_copy.wait()
    div_real = vort(2)
    div_imag = vort(3)
    stream_real = inverse * vort(0)
    stream_imag = inverse * vort(1)
    potential_real = inverse * div_real
    potential_imag = inverse * div_imag
    scale = 1.0 / planet_radius
    thickness = thick_ref[0, 0]
    zeros = jnp.zeros((slots, degrees), f32)
    fields = [
        (-order * potential_imag - derivative(stream_real)) * scale,
        (-order * stream_imag + derivative(potential_real)) * scale,
        div_real * thickness,
        zeros,
        (order * potential_real - derivative(stream_imag)) * scale,
        (order * stream_real + derivative(potential_imag)) * scale,
        div_imag * thickness,
        zeros,
    ]
    for f, field in enumerate(fields):
        for tile in range(tiles):
            start = 128 * tile + 16 * f
            field_ref[start : start + slots, :] = field[:, 128 * tile : 128 * tile + 128]
    first = lax.broadcasted_iota(jnp.int32, (8, 2 * rows), 1) < rows
    for t in range(slots // 2):
        blocks = [
            jnp.concatenate(
                [
                    field_ref[pl.ds(128 * tile + 2 * t + parity, 8, stride=16), :]
                    for tile in range(tiles)
                ],
                axis=1,
            )
            for parity in range(2)
        ]
        left = jnp.concatenate(blocks, axis=0)
        left_low = left - left.astype(bf16).astype(f32)
        left = jnp.concatenate([left, left_low], axis=0).astype(bf16)
        highs, lows = [], []
        for parity in range(2):
            s = 2 * t + parity
            leg_copy(s).wait()
            leg_high, leg_low = halves(jnp.where(valid[s : s + 1], leg_ref[s], 0.0))
            high_ref[s * rows : (s + 1) * rows, :] = leg_high
            low_ref[s * rows : (s + 1) * rows, :] = leg_low
            highs.append(leg_high)
            lows.append(leg_low)
        product = dot_nt(left, jnp.concatenate(highs + lows, axis=0))
        total = product[0:16, 0:128] + product[0:16, 128:256] + product[16:32, 0:128]
        total = jnp.where(first, total[0:8], total[8:16])
        f_ref[8 * t : 8 * t + 8, :] = total
        msg_ref[2 * t : 2 * t + 1, :] = total[2:3]
        msg_ref[2 * t + 1 : 2 * t + 2, :] = total[6:7]
    message = msg_ref[...]
    for copy in range(copies):
        lev_ref[copy * slots : (copy + 1) * slots, :] = message


def table_kernel(owner_ref, table_high_ref, table_low_ref, phase_cos_ref, phase_sin_ref):
    waves, slots = owner_ref.shape
    length = 2.0 * waves * slots
    orders = owner_ref[...].astype(f32)
    offset = lax.broadcasted_iota(jnp.int32, (waves, 128), 1).astype(f32)
    padded = jnp.concatenate([orders, jnp.zeros((waves, 128 - slots), f32)], axis=1)
    by_slot = padded.T
    blocks = phase_cos_ref.shape[0] // (slots // 2)
    block = lax.broadcasted_iota(jnp.int32, (blocks, 128), 0).astype(f32)
    for s in range(slots):
        cosine, sine = cos_sin(orders[:, s : s + 1] * offset, length / 4.0)
        cos_high, cos_low = halves(cosine)
        sin_high, sin_low = halves(-sine)
        rows = slice(s * waves, (s + 1) * waves)
        table_high_ref[rows, 0:128] = cos_high
        table_high_ref[rows, 128:256] = sin_high
        table_low_ref[rows, 0:128] = cos_low
        table_low_ref[rows, 128:256] = sin_low
    for t in range(slots // 2):
        row = jnp.concatenate([by_slot[2 * t : 2 * t + 1, :], by_slot[2 * t + 1 : 2 * t + 2, :]], axis=1)
        cosine, sine = cos_sin(row * block * 128.0, length / 4.0)
        phase_cos_ref[t * blocks : (t + 1) * blocks, :] = cosine
        phase_sin_ref[t * blocks : (t + 1) * blocks, :] = sine


def prefix_kernel(got_ref, f_ref, level_ref, out_ref, ft_ref):
    pairs = f_ref.shape[0] // 8
    copies = got_ref.shape[0] // (2 * pairs)
    level = level_ref[0]
    total = jnp.zeros((2 * pairs, 128), f32)
    for source in range(copies):
        part = got_ref[source * 2 * pairs : (source + 1) * 2 * pairs, :]
        total = total + jnp.where(source < level, part, 0.0)
    ft_ref[0 : 8 * pairs, :] = f_ref[...]
    ft_ref[8 * pairs : 128, :] = jnp.zeros((128 - 8 * pairs, 128), f32)
    for t in range(pairs):
        ft_ref[8 * t + 3 : 8 * t + 4, :] = total[2 * t : 2 * t + 1]
        ft_ref[8 * t + 7 : 8 * t + 8, :] = total[2 * t + 1 : 2 * t + 2]
    turned = ft_ref[...].T
    out_ref[...] = turned[0:64] + pltpu.roll(turned[64:128], 64, 1)


def grid_kernel(
    got_ref,
    table_high_ref,
    table_low_ref,
    phase_cos_ref,
    phase_sin_ref,
    q_ref,
    above_ref,
    below_ref,
    sine_ref,
    weight_ref,
    thick_ref,
    out_ref,
):
    waves = got_ref.shape[0]
    pairs = 5
    blocks = phase_cos_ref.shape[0] // pairs
    used = q_ref.shape[0] // 8
    got = got_ref[...]
    stacked = jnp.concatenate([got, pltpu.roll(got, 64, 1)], axis=0).T
    sign = jnp.where(lax.broadcasted_iota(jnp.int32, (8, 128), 0) < 4, -1.0, 1.0)
    plain = [stacked[8 * t : 8 * t + 8] for t in range(pairs)]
    swapped = [pltpu.roll(x, 4, 0) * sign for x in plain]
    phase_cos = [[phase_cos_ref[t * blocks + b : t * blocks + b + 1, :] for t in range(pairs)] for b in range(used)]
    phase_sin = [[phase_sin_ref[t * blocks + b : t * blocks + b + 1, :] for t in range(pairs)] for b in range(used)]
    turned = jnp.concatenate(
        [
            jnp.concatenate(
                [plain[t] * phase_cos[b][t] + swapped[t] * phase_sin[b][t] for t in range(pairs)], axis=1
            )
            for b in range(used)
        ],
        axis=0,
    )
    table_high = table_high_ref[...]
    table_low = table_low_ref[...]
    grid = three_products(turned, table_high, table_low, dot_nn)
    length = 128.0 * used
    lon_step = 2.0 * math.pi / length
    lat_step = 2.0 * math.pi / length
    sine = sine_ref[0]
    metric = 1.0 - sine * sine
    weight = -weight_ref[0] * (2.0 / length)
    zonal_factor = weight / (metric * (2.0 * lon_step))
    merid_factor = weight / (metric * (2.0 * lat_step))
    vertical_factor = weight / (2.0 * thick_ref[0])
    lane = lax.broadcasted_iota(jnp.int32, (8, 128), 1)
    east, other, merid = [], [], []
    for b in range(used):
        q = q_ref[pl.ds(b, 8, stride=used), :]
        above = above_ref[pl.ds(b, 8, stride=used), :]
        below = below_ref[pl.ds(b, 8, stride=used), :]
        field = grid[8 * b : 8 * b + 4, 0:128] + grid[8 * b + 4 : 8 * b + 8, 128:256]
        east.append(field[0:1] * q)
        merid.append(field[1:2] * q)
        other.append((field[3:4] * (above - below) - field[2:3] * (q + below)) * vertical_factor)
    ahead = [pltpu.roll(z, 127, 1) for z in east]
    behind = [pltpu.roll(z, 1, 1) for z in east]
    rest = []
    for b in range(used):
        right = jnp.where(lane == 127, ahead[(b + 1) % used], ahead[b])
        left = jnp.where(lane == 0, behind[(b - 1) % used], behind[b])
        rest.append(other[b] + zonal_factor * (right - left))
    values = jnp.concatenate(rest + merid, axis=0)
    along_cos = three_products(values, table_high[:, 0:128], table_low[:, 0:128], dot_nt)
    along_sin = three_products(values, table_high[:, 128:256], table_low[:, 128:256], dot_nt)
    for kind in range(2):
        stack = []
        for t in range(pairs):
            cos_total = jnp.zeros((8, 128), f32)
            sin_total = jnp.zeros((8, 128), f32)
            for b in range(used):
                row = 8 * (kind * used + b)
                c = along_cos[row : row + 8, 128 * t : 128 * t + 128]
                s = along_sin[row : row + 8, 128 * t : 128 * t + 128]
                cos_total = cos_total + phase_cos[b][t] * c + phase_sin[b][t] * s
                sin_total = sin_total + phase_cos[b][t] * s - phase_sin[b][t] * c
            stack += [cos_total, sin_total]
        stack.append(jnp.full((128 - 16 * pairs, 128), merid_factor, f32))
        sent = jnp.concatenate(stack, axis=0).T
        for parity in range(2):
            out_ref[pl.ds(kind * 2 + parity, waves, stride=4), :] = sent[parity * 64 : parity * 64 + waves]


def result_kernel(got_ref, high_ref, low_ref, out_ref):
    degrees = high_ref.shape[1]
    rows = got_ref.shape[0] // 4
    slots = high_ref.shape[0] // rows
    tiles = degrees // 128
    zero_row = jnp.zeros((1, 128), f32)
    parts = []
    for parity in range(2):
        rest = got_ref[pl.ds(parity, rows, stride=4), :]
        merid = got_ref[pl.ds(2 + parity, rows, stride=4), :]
        factor = rest[:, 80:81]
        north = jnp.concatenate([merid[1:], zero_row], axis=0)
        south = jnp.concatenate([zero_row, merid[:-1]], axis=0)
        parts.append(rest + factor * (north - south))
    stacked = jnp.concatenate(parts, axis=0).T
    first = lax.broadcasted_iota(jnp.int32, (16, 2 * rows), 1) < rows
    for t in range(slots // 2):
        block = stacked[16 * t : 16 * t + 16]
        left = jnp.concatenate([jnp.where(first, block, 0.0), jnp.where(first, 0.0, block)], axis=0)
        pair = slice(2 * t * rows, 2 * (t + 1) * rows)
        product = three_products(left, high_ref[pair, :], low_ref[pair, :], dot_nn)
        for parity in range(2):
            s = 2 * t + parity
            for part in range(2):
                row = parity * 16 + part * 8
                kept = product[row : row + 8]
                for tile in range(tiles):
                    start = (part * slots + s) * tiles + tile
                    out_ref[pl.ds(start, 8, stride=2 * slots * tiles), :] = kept[:, 128 * tile : 128 * tile + 128]


def local(x):
    return x if INTERPRET else pltpu.with_memory_space_constraint(x, pltpu.VMEM)


def shaped(shape, dtype=f32):
    return jax.ShapeDtypeStruct(shape, dtype) if INTERPRET else pltpu.VMEM(shape, dtype)


def shards(vort_div, legendre, owner_map, lat_sine, quad_weight, thickness, tracers):
    slots, rows, degrees = legendre.shape
    waves = lax.axis_size("wave")
    levels = lax.axis_size("lev")
    count, _, _, length = tracers.shape
    call = lambda kernel, **kw: pl.pallas_call(kernel, interpret=INTERPRET, **kw)
    up = [(i, i + 1) for i in range(levels - 1)]
    down = [(b, a) for a, b in up]
    above = lax.ppermute(tracers, "lev", up)
    below = lax.ppermute(tracers, "lev", down)
    owner = owner_map
    if INTERPRET:
        owner = jnp.concatenate([owner_map, lax.axis_index("wave").reshape(1)])
    level = lax.axis_index("lev").astype(jnp.int32).reshape(1)
    fourier, message, leg_high, leg_low = call(
        winds_kernel,
        name="winds",
        in_specs=[hbm, hbm, hbm, hbm],
        out_specs=(vmem, vmem, vmem, vmem),
        out_shape=(
            shaped((4 * slots, 128)),
            shaped((levels * slots, 128)),
            shaped((slots * rows, degrees), bf16),
            shaped((slots * rows, degrees), bf16),
        ),
        scratch_shapes=[
            pltpu.VMEM((4 * slots * degrees // 128, 128), f32),
            pltpu.VMEM((slots, rows, degrees), f32),
            pltpu.SMEM(owner.shape, jnp.int32),
            pltpu.SMEM((1, 1), f32),
            pltpu.VMEM((degrees, 128), f32),
            pltpu.VMEM((slots, 128), f32),
            pltpu.SemaphoreType.DMA((3,)),
            pltpu.SemaphoreType.DMA((slots,)),
        ],
    )(vort_div.reshape(4 * slots * degrees // 128, 128), legendre, owner, thickness.reshape(1, 1))
    totals = lax.all_to_all(
        message.reshape(levels, 1, slots * 128), "lev", split_axis=0, concat_axis=0, tiled=True
    ).reshape(levels * slots, 128)
    table_high, table_low, phase_cos, phase_sin = call(
        table_kernel,
        name="tables",
        in_specs=[vmem],
        out_specs=(vmem, vmem, vmem, vmem),
        out_shape=(
            shaped((waves * slots, 256), bf16),
            shaped((waves * slots, 256), bf16),
            shaped((slots // 2 * 16, 128)),
            shaped((slots // 2 * 16, 128)),
        ),
    )(local(owner_map.reshape(waves, slots)))
    sent = call(
        prefix_kernel,
        name="prefix",
        in_specs=[vmem, vmem, smem],
        out_specs=vmem,
        out_shape=shaped((rows, 128)),
        scratch_shapes=[pltpu.VMEM((128, 128), f32)],
    )(local(totals), local(fourier), level)
    got = lax.all_to_all(
        sent.reshape(rows, 1, 128), "wave", split_axis=0, concat_axis=0, tiled=True
    ).reshape(waves, 128)
    flat = lambda x: local(x.reshape(count * length // 128, 128))
    spectra = call(
        grid_kernel,
        name="grid",
        in_specs=[vmem] * 8 + [smem] * 3,
        out_specs=vmem,
        out_shape=shaped((waves * 4, 128)),
    )(
        local(got),
        local(table_high),
        local(table_low),
        local(phase_cos),
        local(phase_sin),
        flat(tracers),
        flat(above),
        flat(below),
        lat_sine,
        quad_weight,
        thickness,
    )
    back = lax.all_to_all(
        spectra.reshape(waves, 4, 128), "wave", split_axis=0, concat_axis=0, tiled=True
    ).reshape(rows * 4, 128)
    result = call(
        result_kernel,
        name="result",
        in_specs=[vmem, vmem, vmem],
        out_specs=vmem,
        out_shape=jax.ShapeDtypeStruct((count * 2 * slots * degrees // 128, 128), f32),
    )(local(back), local(leg_high), local(leg_low))
    return result.reshape(count, 2, 1, slots, degrees)


def solution(mesh):
    placed = (
        P(None, "lev", "wave", None),
        P("wave", None, None),
        P(),
        P("wave"),
        P("wave"),
        P("lev"),
        P(None, "lev", "wave", None),
    )

    return jax.shard_map(
        shards,
        mesh=mesh,
        in_specs=placed,
        out_specs=P(None, None, "lev", "wave", None),
        check_vma=False,
    )
```

```python
import math

import jax
import jax.numpy as jnp
from jax import lax
from jax.experimental import pallas as pl
from jax.experimental.pallas import tpu as pltpu
from jax.sharding import PartitionSpec as P


planet_radius = 20.0
INTERPRET = False
f32 = jnp.float32
bf16 = jnp.bfloat16

vmem = pl.BlockSpec(memory_space=pltpu.VMEM)
hbm = pl.BlockSpec(memory_space=pltpu.HBM)
smem = pl.BlockSpec(memory_space=pltpu.SMEM)


def halves(x):
    high = x.astype(bf16)
    low = (x - high.astype(f32)).astype(bf16)
    return high, low


def dot_nn(left, right):
    return lax.dot_general(left, right, (((1,), (0,)), ((), ())), preferred_element_type=f32)


def dot_nt(left, right):
    return lax.dot_general(left, right, (((1,), (1,)), ((), ())), preferred_element_type=f32)


def three_products(left, right_high, right_low, dot):
    rows = left.shape[0]
    high, low = halves(left)
    both = dot(jnp.concatenate([high, low], axis=0), right_high)
    return both[:rows] + both[rows:] + dot(high, right_low)


def cos_sin(steps, quarter):
    turns = jnp.floor(steps * (1.0 / quarter) + 0.5)
    angle = (steps - turns * quarter) * (0.5 * math.pi / quarter)
    z = angle * angle
    sine = ((-1.9515295891e-4 * z + 8.3321608736e-3) * z - 1.6666654611e-1) * z * angle + angle
    cosine = (
        (2.443315711809948e-5 * z - 1.388731625493765e-3) * z + 4.166664568298827e-2
    ) * z * z - 0.5 * z + 1.0
    turn = turns.astype(jnp.int32)
    odd = (turn & 1) == 1
    first = jnp.where(odd, sine, cosine)
    second = jnp.where(odd, cosine, sine)
    return (
        jnp.where(((turn + 1) & 2) == 2, -first, first),
        jnp.where((turn & 2) == 2, -second, second),
    )


def own_orders(owner_ref, slots):
    start = lax.axis_index("wave") * slots if not INTERPRET else owner_ref[owner_ref.shape[0] - 1] * slots
    return [owner_ref[start + s] for s in range(slots)]


def winds_kernel(
    vort_hbm,
    leg_hbm,
    owner_hbm,
    thick_hbm,
    f_ref,
    lev_ref,
    high_ref,
    low_ref,
    vort_ref,
    leg_ref,
    owner_ref,
    thick_ref,
    field_ref,
    msg_ref,
    sem,
):
    slots, rows, degrees = leg_ref.shape
    copies = lev_ref.shape[0] // slots
    tiles = degrees // 128
    vort_copy = pltpu.make_async_copy(vort_hbm, vort_ref, sem.at[0])
    owner_copy = pltpu.make_async_copy(owner_hbm, owner_ref, sem.at[1])
    thick_copy = pltpu.make_async_copy(thick_hbm, thick_ref, sem.at[2])
    owner_copy.start(priority=1)
    thick_copy.start(priority=1)
    vort_copy.start(priority=1)

    leg_copy = pltpu.make_async_copy(leg_hbm, leg_ref, sem.at[3])
    leg_copy.start()
    owner_copy.wait()
    own = own_orders(owner_ref, slots)
    row = lax.broadcasted_iota(jnp.int32, (slots, degrees), 0)
    order = jnp.zeros((slots, degrees), f32)
    for s in range(slots):
        order = jnp.where(row == s, own[s].astype(f32), order)

    def vort(part):
        start = part * slots * tiles
        return jnp.concatenate(
            [vort_ref[pl.ds(start + tile, slots, stride=tiles), :] for tile in range(tiles)], axis=1
        )

    degree = lax.broadcasted_iota(jnp.int32, (slots, degrees), 1).astype(f32)

    def coupling_at(n):
        ratio = jnp.maximum(n * n - order * order, 0.0) / jnp.maximum(4.0 * n * n - 1.0, 1.0)
        return jnp.where(n > order, jnp.sqrt(ratio), 0.0)

    coupling = coupling_at(degree)
    last = degree == degrees - 1
    coupling_next = jnp.where(last, 0.0, coupling_at(degree + 1.0))
    lower_factor = -(degree - 1.0) * coupling
    upper_factor = (degree + 2.0) * coupling_next
    inverse = jnp.where(
        degree > 0, -planet_radius * planet_radius / jnp.maximum(degree * (degree + 1.0), 1.0), 0.0
    )
    valid = degree >= order

    def derivative(field):
        lower = jnp.where(degree == 0, 0.0, pltpu.roll(field, 1, 1))
        upper = jnp.where(last, 0.0, pltpu.roll(field, degrees - 1, 1))
        return lower_factor * lower + upper_factor * upper

    vort_copy.wait()
    thick_copy.wait()
    leg_copy.wait()
    div_real = vort(2)
    div_imag = vort(3)
    stream_real = inverse * vort(0)
    stream_imag = inverse * vort(1)
    potential_real = inverse * div_real
    potential_imag = inverse * div_imag
    scale = 1.0 / planet_radius
    thickness = thick_ref[0, 0]
    zeros = jnp.zeros((slots, degrees), f32)
    fields = [
        (-order * potential_imag - derivative(stream_real)) * scale,
        (-order * stream_imag + derivative(potential_real)) * scale,
        div_real * thickness,
        zeros,
        (order * potential_real - derivative(stream_imag)) * scale,
        (order * stream_real + derivative(potential_imag)) * scale,
        div_imag * thickness,
        zeros,
    ]
    for f, field in enumerate(fields):
        for tile in range(tiles):
            start = 128 * tile + 16 * f
            field_ref[start : start + slots, :] = field[:, 128 * tile : 128 * tile + 128]
    first = lax.broadcasted_iota(jnp.int32, (8, 2 * rows), 1) < rows
    for t in range(slots // 2):
        blocks = [
            jnp.concatenate(
                [
                    field_ref[pl.ds(128 * tile + 2 * t + parity, 8, stride=16), :]
                    for tile in range(tiles)
                ],
                axis=1,
            )
            for parity in range(2)
        ]
        left = jnp.concatenate(blocks, axis=0)
        left_low = left - left.astype(bf16).astype(f32)
        left = jnp.concatenate([left, left_low], axis=0).astype(bf16)
        highs, lows = [], []
        for parity in range(2):
            s = 2 * t + parity
            leg_high, leg_low = halves(jnp.where(valid[s : s + 1], leg_ref[s], 0.0))
            high_ref[s * rows : (s + 1) * rows, :] = leg_high
            low_ref[s * rows : (s + 1) * rows, :] = leg_low
            highs.append(leg_high)
            lows.append(leg_low)
        product = dot_nt(left, jnp.concatenate(highs + lows, axis=0))
        total = product[0:16, 0:128] + product[0:16, 128:256] + product[16:32, 0:128]
        total = jnp.where(first, total[0:8], total[8:16])
        f_ref[8 * t : 8 * t + 8, :] = total
        msg_ref[2 * t : 2 * t + 1, :] = total[2:3]
        msg_ref[2 * t + 1 : 2 * t + 2, :] = total[6:7]
    message = msg_ref[...]
    for copy in range(copies):
        lev_ref[copy * slots : (copy + 1) * slots, :] = message


def table_kernel(
    owner_ref,
    sine_ref,
    weight_ref,
    thick_ref,
    table_high_ref,
    table_low_ref,
    phase_cos_ref,
    phase_sin_ref,
    factor_ref,
):
    waves, slots = owner_ref.shape
    length = 2.0 * waves * slots
    orders = owner_ref[...].astype(f32)
    offset = lax.broadcasted_iota(jnp.int32, (waves, 128), 1).astype(f32)
    padded = jnp.concatenate([orders, jnp.zeros((waves, 128 - slots), f32)], axis=1)
    by_slot = padded.T
    blocks = phase_cos_ref.shape[0] // (slots // 2)
    block = lax.broadcasted_iota(jnp.int32, (blocks, 128), 0).astype(f32)
    for s in range(slots):
        cosine, sine = cos_sin(orders[:, s : s + 1] * offset, length / 4.0)
        cos_high, cos_low = halves(cosine)
        sin_high, sin_low = halves(-sine)
        rows = slice(s * waves, (s + 1) * waves)
        table_high_ref[rows, 0:128] = cos_high
        table_high_ref[rows, 128:256] = sin_high
        table_low_ref[rows, 0:128] = cos_low
        table_low_ref[rows, 128:256] = sin_low
    for t in range(slots // 2):
        row = jnp.concatenate([by_slot[2 * t : 2 * t + 1, :], by_slot[2 * t + 1 : 2 * t + 2, :]], axis=1)
        cosine, sine = cos_sin(row * block * 128.0, length / 4.0)
        phase_cos_ref[t * blocks : (t + 1) * blocks, :] = cosine
        phase_sin_ref[t * blocks : (t + 1) * blocks, :] = sine
    step = 2.0 * math.pi / length
    sine = sine_ref[0]
    weight = jnp.full((8, 128), -weight_ref[0] * (2.0 / length), f32)
    slope = weight / ((1.0 - sine * sine) * (2.0 * step))
    factor_ref[0:8, :] = slope
    factor_ref[8:16, :] = slope
    factor_ref[16:24, :] = weight / (2.0 * thick_ref[0])


def prefix_kernel(got_ref, f_ref, *rest):
    level_ref, out_ref, ft_ref = rest if INTERPRET else (None, *rest)
    level = level_ref[0] if INTERPRET else lax.axis_index("lev")
    pairs = f_ref.shape[0] // 8
    depth = got_ref.shape[0] // (2 * pairs)
    half = level // depth
    own_sum = jnp.zeros((2 * pairs, 128), f32)
    all_sum = jnp.zeros((2 * pairs, 128), f32)
    for source in range(depth):
        part = got_ref[source * 2 * pairs : (source + 1) * 2 * pairs, :]
        own_sum = own_sum + jnp.where(source < level - half * depth, part, 0.0)
        all_sum = all_sum + part
    to_upper = jnp.where(half == 0, all_sum, 0.0)
    blocks = []
    for block, total in enumerate((own_sum, to_upper)):
        start = 128 * block
        if block == 0:
            ft_ref[start : start + 8 * pairs, :] = f_ref[...]
            ft_ref[start + 8 * pairs : start + 128, :] = jnp.zeros((128 - 8 * pairs, 128), f32)
        else:
            ft_ref[start : start + 128, :] = jnp.zeros((128, 128), f32)
        for t in range(pairs):
            row = start + 8 * t
            ft_ref[row + 3 : row + 4, :] = total[2 * t : 2 * t + 1]
            ft_ref[row + 7 : row + 8, :] = total[2 * t + 1 : 2 * t + 2]
        turned = ft_ref[start : start + 128, :].T
        blocks.append(turned[0:64] + pltpu.roll(turned[64:128], 64, 1))
    own_block, other_block = blocks
    out_ref[0:64, :] = jnp.where(half == 0, own_block, other_block)
    out_ref[64:128, :] = jnp.where(half == 0, other_block, own_block)


def grid_kernel(
    got_ref,
    table_high_ref,
    table_low_ref,
    phase_cos_ref,
    phase_sin_ref,
    q_ref,
    above_ref,
    below_ref,
    factor_ref,
    out_ref,
):
    waves = got_ref.shape[0] // 2
    pairs = 5
    blocks = phase_cos_ref.shape[0] // pairs
    used = q_ref.shape[0] // 8
    got = got_ref[0:waves, :] + got_ref[waves : 2 * waves, :]
    stacked = jnp.concatenate([got, pltpu.roll(got, 64, 1)], axis=0).T
    sign = jnp.where(lax.broadcasted_iota(jnp.int32, (8, 128), 0) < 4, -1.0, 1.0)
    plain = [stacked[8 * t : 8 * t + 8] for t in range(pairs)]
    swapped = [pltpu.roll(x, 4, 0) * sign for x in plain]
    phase_cos = [[phase_cos_ref[t * blocks + b : t * blocks + b + 1, :] for t in range(pairs)] for b in range(used)]
    phase_sin = [[phase_sin_ref[t * blocks + b : t * blocks + b + 1, :] for t in range(pairs)] for b in range(used)]
    turned = jnp.concatenate(
        [
            jnp.concatenate(
                [plain[t] * phase_cos[b][t] + swapped[t] * phase_sin[b][t] for t in range(pairs)], axis=1
            )
            for b in range(used)
        ],
        axis=0,
    )
    table_high = table_high_ref[...]
    table_low = table_low_ref[...]
    grid = three_products(turned, table_high, table_low, dot_nn)
    zonal_factor = factor_ref[0:8, :]
    merid_factor = factor_ref[8:16, :]
    vertical_factor = factor_ref[16:24, :]
    lane = lax.broadcasted_iota(jnp.int32, (8, 128), 1)
    east, other, merid = [], [], []
    for b in range(used):
        q = q_ref[pl.ds(b, 8, stride=used), :]
        above = above_ref[pl.ds(b, 8, stride=used), :]
        below = below_ref[pl.ds(b, 8, stride=used), :]
        field = grid[8 * b : 8 * b + 4, 0:128] + grid[8 * b + 4 : 8 * b + 8, 128:256]
        east.append(field[0:1] * q)
        merid.append(field[1:2] * q)
        other.append((field[3:4] * (above - below) - field[2:3] * (q + below)) * vertical_factor)
    ahead = [pltpu.roll(z, 127, 1) for z in east]
    behind = [pltpu.roll(z, 1, 1) for z in east]
    rest = []
    for b in range(used):
        right = jnp.where(lane == 127, ahead[(b + 1) % used], ahead[b])
        left = jnp.where(lane == 0, behind[(b - 1) % used], behind[b])
        rest.append(other[b] + zonal_factor * (right - left))
    values = jnp.concatenate(rest + merid, axis=0)
    along_cos = three_products(values, table_high[:, 0:128], table_low[:, 0:128], dot_nt)
    along_sin = three_products(values, table_high[:, 128:256], table_low[:, 128:256], dot_nt)
    for kind in range(2):
        stack = []
        for t in range(pairs):
            cos_total = jnp.zeros((8, 128), f32)
            sin_total = jnp.zeros((8, 128), f32)
            for b in range(used):
                row = 8 * (kind * used + b)
                c = along_cos[row : row + 8, 128 * t : 128 * t + 128]
                s = along_sin[row : row + 8, 128 * t : 128 * t + 128]
                cos_total = cos_total + phase_cos[b][t] * c + phase_sin[b][t] * s
                sin_total = sin_total + phase_cos[b][t] * s - phase_sin[b][t] * c
            stack += [cos_total, sin_total]
        stack += [merid_factor] * (16 - 2 * pairs)
        sent = jnp.concatenate(stack, axis=0).T
        for parity in range(2):
            out_ref[pl.ds(kind * 2 + parity, waves, stride=4), :] = sent[parity * 64 : parity * 64 + waves]


def result_kernel(got_ref, high_ref, low_ref, out_ref):
    degrees = high_ref.shape[1]
    rows = got_ref.shape[0] // 4
    slots = high_ref.shape[0] // rows
    tiles = degrees // 128
    zero_row = jnp.zeros((1, 128), f32)
    parts = []
    for parity in range(2):
        rest = got_ref[pl.ds(parity, rows, stride=4), :]
        merid = got_ref[pl.ds(2 + parity, rows, stride=4), :]
        factor = rest[:, 80:81]
        north = jnp.concatenate([merid[1:], zero_row], axis=0)
        south = jnp.concatenate([zero_row, merid[:-1]], axis=0)
        parts.append(rest + factor * (north - south))
    stacked = jnp.concatenate(parts, axis=0).T
    first = lax.broadcasted_iota(jnp.int32, (16, 2 * rows), 1) < rows
    for t in range(slots // 2):
        block = stacked[16 * t : 16 * t + 16]
        left = jnp.concatenate([jnp.where(first, block, 0.0), jnp.where(first, 0.0, block)], axis=0)
        pair = slice(2 * t * rows, 2 * (t + 1) * rows)
        product = three_products(left, high_ref[pair, :], low_ref[pair, :], dot_nn)
        for parity in range(2):
            s = 2 * t + parity
            for part in range(2):
                row = parity * 16 + part * 8
                kept = product[row : row + 8]
                for tile in range(tiles):
                    start = (part * slots + s) * tiles + tile
                    out_ref[pl.ds(start, 8, stride=2 * slots * tiles), :] = kept[:, 128 * tile : 128 * tile + 128]


def local(x):
    return x if INTERPRET else pltpu.with_memory_space_constraint(x, pltpu.VMEM)


def shaped(shape, dtype=f32):
    return jax.ShapeDtypeStruct(shape, dtype) if INTERPRET else pltpu.VMEM(shape, dtype)


def shards(vort_div, legendre, owner_map, lat_sine, quad_weight, thickness, tracers):
    slots, rows, degrees = legendre.shape
    waves = lax.axis_size("wave")
    levels = lax.axis_size("lev")
    count, _, _, length = tracers.shape
    call = lambda kernel, **kw: pl.pallas_call(kernel, interpret=INTERPRET, **kw)
    up = [(i, i + 1) for i in range(levels - 1)]
    down = [(b, a) for a, b in up]
    above = lax.ppermute(tracers, "lev", up)
    below = lax.ppermute(tracers, "lev", down)
    owner = owner_map
    if INTERPRET:
        owner = jnp.concatenate([owner_map, lax.axis_index("wave").reshape(1)])
    depth = levels // 2
    columns = [[half * depth + z for z in range(depth)] for half in range(2)]
    planes = [
        [w * levels + half * depth + z for half in range(2) for w in range(waves)] for z in range(depth)
    ]
    level = (lax.axis_index("lev").reshape(1),) if INTERPRET else ()
    fourier, message, leg_high, leg_low = call(
        winds_kernel,
        name="winds",
        in_specs=[hbm, hbm, hbm, hbm],
        out_specs=(vmem, vmem, vmem, vmem),
        out_shape=(
            shaped((4 * slots, 128)),
            shaped((depth * slots, 128)),
            shaped((slots * rows, degrees), bf16),
            shaped((slots * rows, degrees), bf16),
        ),
        scratch_shapes=[
            pltpu.VMEM((4 * slots * degrees // 128, 128), f32),
            pltpu.VMEM((slots, rows, degrees), f32),
            pltpu.SMEM(owner.shape, jnp.int32),
            pltpu.SMEM((1, 1), f32),
            pltpu.VMEM((degrees, 128), f32),
            pltpu.VMEM((slots, 128), f32),
            pltpu.SemaphoreType.DMA((4,)),
        ],
    )(vort_div.reshape(4 * slots * degrees // 128, 128), legendre, owner, thickness.reshape(1, 1))
    totals = lax.all_to_all(
        message.reshape(depth, 1, slots * 128),
        "lev",
        split_axis=0,
        concat_axis=0,
        tiled=True,
        axis_index_groups=columns,
    ).reshape(depth * slots, 128)
    table_high, table_low, phase_cos, phase_sin, factors = call(
        table_kernel,
        name="tables",
        in_specs=[vmem, smem, smem, smem],
        out_specs=(vmem, vmem, vmem, vmem, vmem),
        out_shape=(
            shaped((waves * slots, 256), bf16),
            shaped((waves * slots, 256), bf16),
            shaped((slots // 2 * 16, 128)),
            shaped((slots // 2 * 16, 128)),
            shaped((24, 128)),
        ),
    )(local(owner_map.reshape(waves, slots)), lat_sine, quad_weight, thickness)
    sent = call(
        prefix_kernel,
        name="prefix",
        in_specs=[vmem, vmem] + [smem] * len(level),
        out_specs=vmem,
        out_shape=shaped((2 * rows, 128)),
        scratch_shapes=[pltpu.VMEM((256, 128), f32)],
    )(local(totals), local(fourier), *level)
    got = lax.all_to_all(
        sent.reshape(2 * rows, 1, 128),
        ("wave", "lev"),
        split_axis=0,
        concat_axis=0,
        tiled=True,
        axis_index_groups=planes,
    ).reshape(2 * waves, 128)
    flat = lambda x: local(x.reshape(count * length // 128, 128))
    spectra = call(
        grid_kernel,
        name="grid",
        in_specs=[vmem] * 9,
        out_specs=vmem,
        out_shape=shaped((waves * 4, 128)),
    )(
        local(got),
        local(table_high),
        local(table_low),
        local(phase_cos),
        local(phase_sin),
        flat(tracers),
        flat(above),
        flat(below),
        local(factors),
    )
    back = lax.all_to_all(
        spectra.reshape(waves, 4, 128), "wave", split_axis=0, concat_axis=0, tiled=True
    ).reshape(rows * 4, 128)
    result = call(
        result_kernel,
        name="result",
        in_specs=[vmem, vmem, vmem],
        out_specs=vmem,
        out_shape=jax.ShapeDtypeStruct((count * 2 * slots * degrees // 128, 128), f32),
    )(local(back), local(leg_high), local(leg_low))
    return result.reshape(count, 2, 1, slots, degrees)


def solution(mesh):
    placed = (
        P(None, "lev", "wave", None),
        P("wave", None, None),
        P(),
        P("wave"),
        P("wave"),
        P("lev"),
        P(None, "lev", "wave", None),
    )

    return jax.shard_map(
        shards,
        mesh=mesh,
        in_specs=placed,
        out_specs=P(None, None, "lev", "wave", None),
        check_vma=False,
    )
```

```python
import functools
import math

import jax
import jax.numpy as jnp
from jax import lax
from jax.experimental import pallas as pl
from jax.experimental.pallas import tpu as pltpu
from jax.sharding import PartitionSpec as P


planet_radius = 20.0
INTERPRET = False
f32 = jnp.float32
bf16 = jnp.bfloat16

vmem = pl.BlockSpec(memory_space=pltpu.VMEM)
hbm = pl.BlockSpec(memory_space=pltpu.HBM)
smem = pl.BlockSpec(memory_space=pltpu.SMEM)


def halves(x):
    high = x.astype(bf16)
    low = (x - high.astype(f32)).astype(bf16)
    return high, low


def dot_nn(left, right):
    return lax.dot_general(left, right, (((1,), (0,)), ((), ())), preferred_element_type=f32)


def dot_nt(left, right):
    return lax.dot_general(left, right, (((1,), (1,)), ((), ())), preferred_element_type=f32)


def three_products(left, right_high, right_low, dot):
    rows = left.shape[0]
    high, low = halves(left)
    both = dot(jnp.concatenate([high, low], axis=0), right_high)
    return both[:rows] + both[rows:] + dot(high, right_low)


def cos_sin(steps, quarter):
    turns = jnp.floor(steps * (1.0 / quarter) + 0.5)
    angle = (steps - turns * quarter) * (0.5 * math.pi / quarter)
    z = angle * angle
    sine = ((-1.9515295891e-4 * z + 8.3321608736e-3) * z - 1.6666654611e-1) * z * angle + angle
    cosine = (
        (2.443315711809948e-5 * z - 1.388731625493765e-3) * z + 4.166664568298827e-2
    ) * z * z - 0.5 * z + 1.0
    turn = turns.astype(jnp.int32)
    odd = (turn & 1) == 1
    first = jnp.where(odd, sine, cosine)
    second = jnp.where(odd, cosine, sine)
    return (
        jnp.where(((turn + 1) & 2) == 2, -first, first),
        jnp.where((turn & 2) == 2, -second, second),
    )


def own_orders(owner_ref, slots):
    start = lax.axis_index("wave") * slots if not INTERPRET else owner_ref[owner_ref.shape[0] - 1] * slots
    return [owner_ref[start + s] for s in range(slots)]


def winds_kernel(
    vort_hbm,
    leg_hbm,
    owner_hbm,
    thick_hbm,
    f_ref,
    lev_ref,
    high_ref,
    low_ref,
    vort_ref,
    leg_ref,
    owner_ref,
    thick_ref,
    field_ref,
    msg_ref,
    sem,
):
    slots, rows, degrees = leg_ref.shape
    copies = lev_ref.shape[0] // slots
    tiles = degrees // 128
    vort_copy = pltpu.make_async_copy(vort_hbm, vort_ref, sem.at[0])
    owner_copy = pltpu.make_async_copy(owner_hbm, owner_ref, sem.at[1])
    thick_copy = pltpu.make_async_copy(thick_hbm, thick_ref, sem.at[2])
    owner_copy.start(priority=1)
    thick_copy.start(priority=1)
    vort_copy.start(priority=1)

    leg_copy = pltpu.make_async_copy(leg_hbm, leg_ref, sem.at[3])
    leg_copy.start()
    owner_copy.wait()
    own = own_orders(owner_ref, slots)
    row = lax.broadcasted_iota(jnp.int32, (slots, degrees), 0)
    order = jnp.zeros((slots, degrees), f32)
    for s in range(slots):
        order = jnp.where(row == s, own[s].astype(f32), order)

    def vort(part):
        start = part * slots * tiles
        return jnp.concatenate(
            [vort_ref[pl.ds(start + tile, slots, stride=tiles), :] for tile in range(tiles)], axis=1
        )

    degree = lax.broadcasted_iota(jnp.int32, (slots, degrees), 1).astype(f32)

    def coupling_at(n):
        ratio = jnp.maximum(n * n - order * order, 0.0) / jnp.maximum(4.0 * n * n - 1.0, 1.0)
        return jnp.where(n > order, jnp.sqrt(ratio), 0.0)

    coupling = coupling_at(degree)
    last = degree == degrees - 1
    coupling_next = jnp.where(last, 0.0, coupling_at(degree + 1.0))
    lower_factor = -(degree - 1.0) * coupling
    upper_factor = (degree + 2.0) * coupling_next
    inverse = jnp.where(
        degree > 0, -planet_radius * planet_radius / jnp.maximum(degree * (degree + 1.0), 1.0), 0.0
    )
    valid = degree >= order

    def derivative(field):
        lower = jnp.where(degree == 0, 0.0, pltpu.roll(field, 1, 1))
        upper = jnp.where(last, 0.0, pltpu.roll(field, degrees - 1, 1))
        return lower_factor * lower + upper_factor * upper

    vort_copy.wait()
    thick_copy.wait()
    leg_copy.wait()
    div_real = vort(2)
    div_imag = vort(3)
    stream_real = inverse * vort(0)
    stream_imag = inverse * vort(1)
    potential_real = inverse * div_real
    potential_imag = inverse * div_imag
    scale = 1.0 / planet_radius
    thickness = thick_ref[0, 0]
    zeros = jnp.zeros((slots, degrees), f32)
    fields = [
        (-order * potential_imag - derivative(stream_real)) * scale,
        (-order * stream_imag + derivative(potential_real)) * scale,
        div_real * thickness,
        zeros,
        (order * potential_real - derivative(stream_imag)) * scale,
        (order * stream_real + derivative(potential_imag)) * scale,
        div_imag * thickness,
        zeros,
    ]
    for f, field in enumerate(fields):
        for tile in range(tiles):
            start = 128 * tile + 16 * f
            field_ref[start : start + slots, :] = field[:, 128 * tile : 128 * tile + 128]
    first = lax.broadcasted_iota(jnp.int32, (8, 2 * rows), 1) < rows
    for t in range(slots // 2):
        blocks = [
            jnp.concatenate(
                [
                    field_ref[pl.ds(128 * tile + 2 * t + parity, 8, stride=16), :]
                    for tile in range(tiles)
                ],
                axis=1,
            )
            for parity in range(2)
        ]
        left = jnp.concatenate(blocks, axis=0)
        left_low = left - left.astype(bf16).astype(f32)
        left = jnp.concatenate([left, left_low], axis=0).astype(bf16)
        highs, lows = [], []
        for parity in range(2):
            s = 2 * t + parity
            leg_high, leg_low = halves(jnp.where(valid[s : s + 1], leg_ref[s], 0.0))
            high_ref[s * rows : (s + 1) * rows, :] = leg_high
            low_ref[s * rows : (s + 1) * rows, :] = leg_low
            highs.append(leg_high)
            lows.append(leg_low)
        product = dot_nt(left, jnp.concatenate(highs + lows, axis=0))
        total = product[0:16, 0:128] + product[0:16, 128:256] + product[16:32, 0:128]
        total = jnp.where(first, total[0:8], total[8:16])
        f_ref[8 * t : 8 * t + 8, :] = total
        msg_ref[2 * t : 2 * t + 1, :] = total[2:3]
        msg_ref[2 * t + 1 : 2 * t + 2, :] = total[6:7]
    message = msg_ref[...]
    for copy in range(copies):
        lev_ref[copy * slots : (copy + 1) * slots, :] = message


def table_kernel(
    owner_ref,
    sine_hbm,
    weight_hbm,
    thick_hbm,
    table_high_ref,
    table_low_ref,
    phase_cos_ref,
    phase_sin_ref,
    factor_ref,
    scalar_ref,
    sem,
):
    waves, slots = owner_ref.shape
    length = 2.0 * waves * slots
    copies = [
        pltpu.make_async_copy(source, scalar_ref.at[pl.ds(i, 1)], sem.at[i])
        for i, source in enumerate((sine_hbm, weight_hbm, thick_hbm))
    ]
    for copy in copies:
        copy.start()
    orders = owner_ref[...].astype(f32)
    offset = lax.broadcasted_iota(jnp.int32, (waves, 128), 1).astype(f32)
    padded = jnp.concatenate([orders, jnp.zeros((waves, 128 - slots), f32)], axis=1)
    by_slot = padded.T
    blocks = phase_cos_ref.shape[0] // (slots // 2)
    block = lax.broadcasted_iota(jnp.int32, (blocks, 128), 0).astype(f32)
    for s in range(slots):
        cosine, sine = cos_sin(orders[:, s : s + 1] * offset, length / 4.0)
        cos_high, cos_low = halves(cosine)
        sin_high, sin_low = halves(-sine)
        rows = slice(s * waves, (s + 1) * waves)
        table_high_ref[rows, 0:128] = cos_high
        table_high_ref[rows, 128:256] = sin_high
        table_low_ref[rows, 0:128] = cos_low
        table_low_ref[rows, 128:256] = sin_low
    for t in range(slots // 2):
        row = jnp.concatenate([by_slot[2 * t : 2 * t + 1, :], by_slot[2 * t + 1 : 2 * t + 2, :]], axis=1)
        cosine, sine = cos_sin(row * block * 128.0, length / 4.0)
        phase_cos_ref[t * blocks : (t + 1) * blocks, :] = cosine
        phase_sin_ref[t * blocks : (t + 1) * blocks, :] = sine
    for copy in copies:
        copy.wait()
    step = 2.0 * math.pi / length
    sine = scalar_ref[0, 0]
    weight = jnp.full((8, 128), -scalar_ref[1, 0] * (2.0 / length), f32)
    slope = weight / ((1.0 - sine * sine) * (2.0 * step))
    factor_ref[0:8, :] = slope
    factor_ref[8:16, :] = slope
    factor_ref[16:24, :] = weight / (2.0 * scalar_ref[2, 0])


def prefix_kernel(got_ref, f_ref, *rest):
    level_ref, out_ref, ft_ref = rest if INTERPRET else (None, *rest)
    level = level_ref[0] if INTERPRET else lax.axis_index("lev")
    pairs = f_ref.shape[0] // 8
    total = jnp.zeros((2 * pairs, 128), f32)
    for source in range(got_ref.shape[0] // (2 * pairs)):
        part = got_ref[source * 2 * pairs : (source + 1) * 2 * pairs, :]
        total = total + jnp.where(source < level, part, 0.0)
    ft_ref[0 : 8 * pairs, :] = f_ref[...]
    ft_ref[8 * pairs : 128, :] = jnp.zeros((128 - 8 * pairs, 128), f32)
    for t in range(pairs):
        ft_ref[8 * t + 3 : 8 * t + 4, :] = total[2 * t : 2 * t + 1]
        ft_ref[8 * t + 7 : 8 * t + 8, :] = total[2 * t + 1 : 2 * t + 2]
    turned = ft_ref[...].T
    out_ref[...] = turned[0:64] + pltpu.roll(turned[64:128], 64, 1)


def grid_kernel(
    got_ref,
    table_high_ref,
    table_low_ref,
    phase_cos_ref,
    phase_sin_ref,
    q_ref,
    above_ref,
    below_ref,
    cross_ref,
    factor_ref,
    *rest,
    depth,
):
    level_ref, out_ref = rest if INTERPRET else (None, *rest)
    level = level_ref[0] if INTERPRET else lax.axis_index("lev")
    first_level = level % depth == 0
    last_level = level % depth == depth - 1
    waves = got_ref.shape[0]
    pairs = 5
    blocks = phase_cos_ref.shape[0] // pairs
    used = q_ref.shape[0] // 8
    got = got_ref[...]
    stacked = jnp.concatenate([got, pltpu.roll(got, 64, 1)], axis=0).T
    sign = jnp.where(lax.broadcasted_iota(jnp.int32, (8, 128), 0) < 4, -1.0, 1.0)
    plain = [stacked[8 * t : 8 * t + 8] for t in range(pairs)]
    swapped = [pltpu.roll(x, 4, 0) * sign for x in plain]
    phase_cos = [[phase_cos_ref[t * blocks + b : t * blocks + b + 1, :] for t in range(pairs)] for b in range(used)]
    phase_sin = [[phase_sin_ref[t * blocks + b : t * blocks + b + 1, :] for t in range(pairs)] for b in range(used)]
    turned = jnp.concatenate(
        [
            jnp.concatenate(
                [plain[t] * phase_cos[b][t] + swapped[t] * phase_sin[b][t] for t in range(pairs)], axis=1
            )
            for b in range(used)
        ],
        axis=0,
    )
    table_high = table_high_ref[...]
    table_low = table_low_ref[...]
    grid = three_products(turned, table_high, table_low, dot_nn)
    zonal_factor = factor_ref[0:8, :]
    merid_factor = factor_ref[8:16, :]
    vertical_factor = factor_ref[16:24, :]
    lane = lax.broadcasted_iota(jnp.int32, (8, 128), 1)
    east, other, merid = [], [], []
    for b in range(used):
        q = q_ref[pl.ds(b, 8, stride=used), :]
        above = above_ref[pl.ds(b, 8, stride=used), :]
        below = below_ref[pl.ds(b, 8, stride=used), :]
        cross = cross_ref[pl.ds(b, 8, stride=used), :]
        above = jnp.where(first_level, cross, above)
        below = jnp.where(last_level, cross, below)
        field = grid[8 * b : 8 * b + 4, 0:128] + grid[8 * b + 4 : 8 * b + 8, 128:256]
        east.append(field[0:1] * q)
        merid.append(field[1:2] * q)
        other.append((field[3:4] * (above - below) - field[2:3] * (q + below)) * vertical_factor)
    ahead = [pltpu.roll(z, 127, 1) for z in east]
    behind = [pltpu.roll(z, 1, 1) for z in east]
    rest = []
    for b in range(used):
        right = jnp.where(lane == 127, ahead[(b + 1) % used], ahead[b])
        left = jnp.where(lane == 0, behind[(b - 1) % used], behind[b])
        rest.append(other[b] + zonal_factor * (right - left))
    values = jnp.concatenate(rest + merid, axis=0)
    along_cos = three_products(values, table_high[:, 0:128], table_low[:, 0:128], dot_nt)
    along_sin = three_products(values, table_high[:, 128:256], table_low[:, 128:256], dot_nt)
    for kind in range(2):
        stack = []
        for t in range(pairs):
            cos_total = jnp.zeros((8, 128), f32)
            sin_total = jnp.zeros((8, 128), f32)
            for b in range(used):
                row = 8 * (kind * used + b)
                c = along_cos[row : row + 8, 128 * t : 128 * t + 128]
                s = along_sin[row : row + 8, 128 * t : 128 * t + 128]
                cos_total = cos_total + phase_cos[b][t] * c + phase_sin[b][t] * s
                sin_total = sin_total + phase_cos[b][t] * s - phase_sin[b][t] * c
            stack += [cos_total, sin_total]
        stack += [merid_factor] * (16 - 2 * pairs)
        sent = jnp.concatenate(stack, axis=0).T
        for parity in range(2):
            out_ref[pl.ds(kind * 2 + parity, waves, stride=4), :] = sent[parity * 64 : parity * 64 + waves]


def result_kernel(got_ref, high_ref, low_ref, out_ref):
    degrees = high_ref.shape[1]
    rows = got_ref.shape[0] // 4
    slots = high_ref.shape[0] // rows
    tiles = degrees // 128
    zero_row = jnp.zeros((1, 128), f32)
    parts = []
    for parity in range(2):
        rest = got_ref[pl.ds(parity, rows, stride=4), :]
        merid = got_ref[pl.ds(2 + parity, rows, stride=4), :]
        factor = rest[:, 80:81]
        north = jnp.concatenate([merid[1:], zero_row], axis=0)
        south = jnp.concatenate([zero_row, merid[:-1]], axis=0)
        parts.append(rest + factor * (north - south))
    stacked = jnp.concatenate(parts, axis=0).T
    first = lax.broadcasted_iota(jnp.int32, (16, 2 * rows), 1) < rows
    for t in range(slots // 2):
        block = stacked[16 * t : 16 * t + 16]
        left = jnp.concatenate([jnp.where(first, block, 0.0), jnp.where(first, 0.0, block)], axis=0)
        pair = slice(2 * t * rows, 2 * (t + 1) * rows)
        product = three_products(left, high_ref[pair, :], low_ref[pair, :], dot_nn)
        for parity in range(2):
            s = 2 * t + parity
            for part in range(2):
                row = parity * 16 + part * 8
                kept = product[row : row + 8]
                for tile in range(tiles):
                    start = (part * slots + s) * tiles + tile
                    out_ref[pl.ds(start, 8, stride=2 * slots * tiles), :] = kept[:, 128 * tile : 128 * tile + 128]


def local(x):
    return x if INTERPRET else pltpu.with_memory_space_constraint(x, pltpu.VMEM)


def shaped(shape, dtype=f32):
    return jax.ShapeDtypeStruct(shape, dtype) if INTERPRET else pltpu.VMEM(shape, dtype)


def shards(vort_div, legendre, owner_map, lat_sine, quad_weight, thickness, tracers):
    slots, rows, degrees = legendre.shape
    waves = lax.axis_size("wave")
    levels = lax.axis_size("lev")
    count, _, _, length = tracers.shape
    call = lambda kernel, **kw: pl.pallas_call(kernel, interpret=INTERPRET, **kw)
    depth = levels // 2
    starts = [half * depth for half in range(2)]
    up = [(h + z, h + (z + 1) % depth) for h in starts for z in range(depth)]
    down = [(b, a) for a, b in up]
    above = lax.ppermute(tracers, "lev", up)
    below = lax.ppermute(tracers, "lev", down)
    around = jnp.where(lax.axis_index("lev") % depth == 0, above, below)
    cross = lax.ppermute(around, "lev", [(0, depth), (levels - 1, depth - 1)])
    owner = owner_map
    if INTERPRET:
        owner = jnp.concatenate([owner_map, lax.axis_index("wave").reshape(1)])
    level = (lax.axis_index("lev").reshape(1),) if INTERPRET else ()
    fourier, message, leg_high, leg_low = call(
        winds_kernel,
        name="winds",
        in_specs=[hbm, hbm, hbm, hbm],
        out_specs=(vmem, vmem, vmem, vmem),
        out_shape=(
            shaped((4 * slots, 128)),
            shaped((levels * slots, 128)),
            shaped((slots * rows, degrees), bf16),
            shaped((slots * rows, degrees), bf16),
        ),
        scratch_shapes=[
            pltpu.VMEM((4 * slots * degrees // 128, 128), f32),
            pltpu.VMEM((slots, rows, degrees), f32),
            pltpu.SMEM(owner.shape, jnp.int32),
            pltpu.SMEM((1, 1), f32),
            pltpu.VMEM((degrees, 128), f32),
            pltpu.VMEM((slots, 128), f32),
            pltpu.SemaphoreType.DMA((4,)),
        ],
    )(vort_div.reshape(4 * slots * degrees // 128, 128), legendre, owner, thickness.reshape(1, 1))
    totals = lax.all_to_all(
        message.reshape(levels, 1, slots * 128), "lev", split_axis=0, concat_axis=0, tiled=True
    ).reshape(levels * slots, 128)
    table_high, table_low, phase_cos, phase_sin, factors = call(
        table_kernel,
        name="tables",
        in_specs=[vmem, hbm, hbm, hbm],
        out_specs=(vmem, vmem, vmem, vmem, vmem),
        scratch_shapes=[pltpu.SMEM((3, 1), f32), pltpu.SemaphoreType.DMA((3,))],
        out_shape=(
            shaped((waves * slots, 256), bf16),
            shaped((waves * slots, 256), bf16),
            shaped((slots // 2 * 16, 128)),
            shaped((slots // 2 * 16, 128)),
            shaped((24, 128)),
        ),
    )(local(owner_map.reshape(waves, slots)), *(x.reshape(1, 1) for x in (lat_sine, quad_weight, thickness)))
    sent = call(
        prefix_kernel,
        name="prefix",
        in_specs=[vmem, vmem] + [smem] * len(level),
        out_specs=vmem,
        out_shape=shaped((rows, 128)),
        scratch_shapes=[pltpu.VMEM((128, 128), f32)],
    )(local(totals), local(fourier), *level)
    got = lax.all_to_all(
        sent.reshape(rows, 1, 128), "wave", split_axis=0, concat_axis=0, tiled=True
    ).reshape(waves, 128)
    flat = lambda x: local(x.reshape(count * length // 128, 128))
    spectra = call(
        functools.partial(grid_kernel, depth=depth),
        name="grid",
        in_specs=[vmem] * 10 + [smem] * len(level),
        out_specs=vmem,
        out_shape=shaped((waves * 4, 128)),
    )(
        local(got),
        local(table_high),
        local(table_low),
        local(phase_cos),
        local(phase_sin),
        flat(tracers),
        flat(above),
        flat(below),
        flat(cross),
        local(factors),
        *level,
    )
    back = lax.all_to_all(
        spectra.reshape(waves, 4, 128), "wave", split_axis=0, concat_axis=0, tiled=True
    ).reshape(rows * 4, 128)
    result = call(
        result_kernel,
        name="result",
        in_specs=[vmem, vmem, vmem],
        out_specs=vmem,
        out_shape=jax.ShapeDtypeStruct((count * 2 * slots * degrees // 128, 128), f32),
    )(local(back), local(leg_high), local(leg_low))
    return result.reshape(count, 2, 1, slots, degrees)


def solution(mesh):
    placed = (
        P(None, "lev", "wave", None),
        P("wave", None, None),
        P(),
        P("wave"),
        P("wave"),
        P("lev"),
        P(None, "lev", "wave", None),
    )

    return jax.shard_map(
        shards,
        mesh=mesh,
        in_specs=placed,
        out_specs=P(None, None, "lev", "wave", None),
        check_vma=False,
    )
```

```python
import math

import jax
import jax.numpy as jnp
from jax import lax
from jax.experimental import pallas as pl
from jax.experimental.pallas import tpu as pltpu
from jax.sharding import PartitionSpec as P


planet_radius = 20.0
INTERPRET = False
f32 = jnp.float32
bf16 = jnp.bfloat16

vmem = pl.BlockSpec(memory_space=pltpu.VMEM)
hbm = pl.BlockSpec(memory_space=pltpu.HBM)
smem = pl.BlockSpec(memory_space=pltpu.SMEM)


def halves(x):
    high = x.astype(bf16)
    low = (x - high.astype(f32)).astype(bf16)
    return high, low


def dot_nn(left, right):
    return lax.dot_general(left, right, (((1,), (0,)), ((), ())), preferred_element_type=f32)


def dot_nt(left, right):
    return lax.dot_general(left, right, (((1,), (1,)), ((), ())), preferred_element_type=f32)


def three_products(left, right_high, right_low, dot):
    rows = left.shape[0]
    high, low = halves(left)
    both = dot(jnp.concatenate([high, low], axis=0), right_high)
    return both[:rows] + both[rows:] + dot(high, right_low)


def cos_sin(steps, quarter):
    turns = jnp.floor(steps * (1.0 / quarter) + 0.5)
    angle = (steps - turns * quarter) * (0.5 * math.pi / quarter)
    z = angle * angle
    sine = ((-1.9515295891e-4 * z + 8.3321608736e-3) * z - 1.6666654611e-1) * z * angle + angle
    cosine = (
        (2.443315711809948e-5 * z - 1.388731625493765e-3) * z + 4.166664568298827e-2
    ) * z * z - 0.5 * z + 1.0
    turn = turns.astype(jnp.int32)
    odd = (turn & 1) == 1
    first = jnp.where(odd, sine, cosine)
    second = jnp.where(odd, cosine, sine)
    return (
        jnp.where(((turn + 1) & 2) == 2, -first, first),
        jnp.where((turn & 2) == 2, -second, second),
    )


def own_orders(owner_ref, slots):
    start = lax.axis_index("wave") * slots if not INTERPRET else owner_ref[owner_ref.shape[0] - 1] * slots
    return [owner_ref[start + s] for s in range(slots)]


def winds_kernel(
    vort_hbm,
    leg_hbm,
    owner_hbm,
    thick_hbm,
    f_ref,
    lev_ref,
    high_ref,
    low_ref,
    vort_ref,
    leg_ref,
    owner_ref,
    thick_ref,
    field_ref,
    msg_ref,
    sem,
):
    slots, rows, degrees = leg_ref.shape
    copies = lev_ref.shape[0] // slots
    tiles = degrees // 128
    vort_copy = pltpu.make_async_copy(vort_hbm, vort_ref, sem.at[0])
    owner_copy = pltpu.make_async_copy(owner_hbm, owner_ref, sem.at[1])
    thick_copy = pltpu.make_async_copy(thick_hbm, thick_ref, sem.at[2])
    owner_copy.start(priority=1)
    thick_copy.start(priority=1)
    vort_copy.start(priority=1)

    leg_copy = pltpu.make_async_copy(leg_hbm, leg_ref, sem.at[3])
    leg_copy.start()
    owner_copy.wait()
    own = own_orders(owner_ref, slots)
    row = lax.broadcasted_iota(jnp.int32, (slots, degrees), 0)
    order = jnp.zeros((slots, degrees), f32)
    for s in range(slots):
        order = jnp.where(row == s, own[s].astype(f32), order)

    def vort(part):
        start = part * slots * tiles
        return jnp.concatenate(
            [vort_ref[pl.ds(start + tile, slots, stride=tiles), :] for tile in range(tiles)], axis=1
        )

    degree = lax.broadcasted_iota(jnp.int32, (slots, degrees), 1).astype(f32)

    def coupling_at(n):
        ratio = jnp.maximum(n * n - order * order, 0.0) / jnp.maximum(4.0 * n * n - 1.0, 1.0)
        return jnp.where(n > order, jnp.sqrt(ratio), 0.0)

    coupling = coupling_at(degree)
    last = degree == degrees - 1
    coupling_next = jnp.where(last, 0.0, coupling_at(degree + 1.0))
    lower_factor = -(degree - 1.0) * coupling
    upper_factor = (degree + 2.0) * coupling_next
    inverse = jnp.where(
        degree > 0, -planet_radius * planet_radius / jnp.maximum(degree * (degree + 1.0), 1.0), 0.0
    )
    valid = degree >= order

    def derivative(field):
        lower = jnp.where(degree == 0, 0.0, pltpu.roll(field, 1, 1))
        upper = jnp.where(last, 0.0, pltpu.roll(field, degrees - 1, 1))
        return lower_factor * lower + upper_factor * upper

    vort_copy.wait()
    thick_copy.wait()
    leg_copy.wait()
    div_real = vort(2)
    div_imag = vort(3)
    stream_real = inverse * vort(0)
    stream_imag = inverse * vort(1)
    potential_real = inverse * div_real
    potential_imag = inverse * div_imag
    scale = 1.0 / planet_radius
    thickness = thick_ref[0, 0]
    zeros = jnp.zeros((slots, degrees), f32)
    fields = [
        (-order * potential_imag - derivative(stream_real)) * scale,
        (-order * stream_imag + derivative(potential_real)) * scale,
        div_real * thickness,
        zeros,
        (order * potential_real - derivative(stream_imag)) * scale,
        (order * stream_real + derivative(potential_imag)) * scale,
        div_imag * thickness,
        zeros,
    ]
    for f, field in enumerate(fields):
        for tile in range(tiles):
            start = 128 * tile + 16 * f
            field_ref[start : start + slots, :] = field[:, 128 * tile : 128 * tile + 128]
    first = lax.broadcasted_iota(jnp.int32, (8, 2 * rows), 1) < rows
    for t in range(slots // 2):
        blocks = [
            jnp.concatenate(
                [
                    field_ref[pl.ds(128 * tile + 2 * t + parity, 8, stride=16), :]
                    for tile in range(tiles)
                ],
                axis=1,
            )
            for parity in range(2)
        ]
        left = jnp.concatenate(blocks, axis=0)
        left_low = left - left.astype(bf16).astype(f32)
        left = jnp.concatenate([left, left_low], axis=0).astype(bf16)
        highs, lows = [], []
        for parity in range(2):
            s = 2 * t + parity
            leg_high, leg_low = halves(jnp.where(valid[s : s + 1], leg_ref[s], 0.0))
            high_ref[s * rows : (s + 1) * rows, :] = leg_high
            low_ref[s * rows : (s + 1) * rows, :] = leg_low
            highs.append(leg_high)
            lows.append(leg_low)
        product = dot_nt(left, jnp.concatenate(highs + lows, axis=0))
        total = product[0:16, 0:128] + product[0:16, 128:256] + product[16:32, 0:128]
        total = jnp.where(first, total[0:8], total[8:16])
        f_ref[8 * t : 8 * t + 8, :] = total
        msg_ref[2 * t : 2 * t + 1, :] = total[2:3]
        msg_ref[2 * t + 1 : 2 * t + 2, :] = total[6:7]
    message = msg_ref[...]
    for copy in range(copies):
        lev_ref[copy * slots : (copy + 1) * slots, :] = message


def table_kernel(
    owner_ref,
    sine_ref,
    weight_ref,
    thick_ref,
    table_high_ref,
    table_low_ref,
    phase_cos_ref,
    phase_sin_ref,
    factor_ref,
):
    waves, slots = owner_ref.shape
    length = 2.0 * waves * slots
    orders = owner_ref[...].astype(f32)
    offset = lax.broadcasted_iota(jnp.int32, (waves, 128), 1).astype(f32)
    padded = jnp.concatenate([orders, jnp.zeros((waves, 128 - slots), f32)], axis=1)
    by_slot = padded.T
    blocks = phase_cos_ref.shape[0] // (slots // 2)
    block = lax.broadcasted_iota(jnp.int32, (blocks, 128), 0).astype(f32)
    for s in range(slots):
        cosine, sine = cos_sin(orders[:, s : s + 1] * offset, length / 4.0)
        cos_high, cos_low = halves(cosine)
        sin_high, sin_low = halves(-sine)
        rows = slice(s * waves, (s + 1) * waves)
        table_high_ref[rows, 0:128] = cos_high
        table_high_ref[rows, 128:256] = sin_high
        table_low_ref[rows, 0:128] = cos_low
        table_low_ref[rows, 128:256] = sin_low
    for t in range(slots // 2):
        row = jnp.concatenate([by_slot[2 * t : 2 * t + 1, :], by_slot[2 * t + 1 : 2 * t + 2, :]], axis=1)
        cosine, sine = cos_sin(row * block * 128.0, length / 4.0)
        phase_cos_ref[t * blocks : (t + 1) * blocks, :] = cosine
        phase_sin_ref[t * blocks : (t + 1) * blocks, :] = sine
    step = 2.0 * math.pi / length
    sine = sine_ref[0]
    weight = jnp.full((8, 128), -weight_ref[0] * (2.0 / length), f32)
    slope = weight / ((1.0 - sine * sine) * (2.0 * step))
    factor_ref[0:8, :] = slope
    factor_ref[8:16, :] = slope
    factor_ref[16:24, :] = weight / (2.0 * thick_ref[0])


def prefix_kernel(got_ref, f_ref, *rest):
    level_ref, out_ref, ft_ref = rest if INTERPRET else (None, *rest)
    level = level_ref[0] if INTERPRET else lax.axis_index("lev")
    pairs = f_ref.shape[0] // 8
    depth = got_ref.shape[0] // (2 * pairs)
    half = level // depth
    own_sum = jnp.zeros((2 * pairs, 128), f32)
    all_sum = jnp.zeros((2 * pairs, 128), f32)
    for source in range(depth):
        part = got_ref[source * 2 * pairs : (source + 1) * 2 * pairs, :]
        own_sum = own_sum + jnp.where(source < level - half * depth, part, 0.0)
        all_sum = all_sum + part
    to_upper = jnp.where(half == 0, all_sum, 0.0)
    blocks = []
    for block, total in enumerate((own_sum, to_upper)):
        start = 128 * block
        if block == 0:
            ft_ref[start : start + 8 * pairs, :] = f_ref[...]
            ft_ref[start + 8 * pairs : start + 128, :] = jnp.zeros((128 - 8 * pairs, 128), f32)
        else:
            ft_ref[start : start + 128, :] = jnp.zeros((128, 128), f32)
        for t in range(pairs):
            row = start + 8 * t
            ft_ref[row + 3 : row + 4, :] = total[2 * t : 2 * t + 1]
            ft_ref[row + 7 : row + 8, :] = total[2 * t + 1 : 2 * t + 2]
        turned = ft_ref[start : start + 128, :].T
        blocks.append(turned[0:64] + pltpu.roll(turned[64:128], 64, 1))
    own_block, other_block = blocks
    out_ref[0:64, :] = jnp.where(half == 0, own_block, other_block)
    out_ref[64:128, :] = jnp.where(half == 0, other_block, own_block)


def grid_kernel(
    got_ref,
    table_high_ref,
    table_low_ref,
    phase_cos_ref,
    phase_sin_ref,
    q_ref,
    above_ref,
    below_ref,
    factor_ref,
    *rest,
):
    level_ref, out_ref = rest if INTERPRET else (None, *rest)
    level = level_ref[0] if INTERPRET else lax.axis_index("lev")
    even = level % 2 == 0
    waves = got_ref.shape[0] // 2
    pairs = 5
    blocks = phase_cos_ref.shape[0] // pairs
    used = q_ref.shape[0] // 8
    got = got_ref[0:waves, :] + got_ref[waves : 2 * waves, :]
    stacked = jnp.concatenate([got, pltpu.roll(got, 64, 1)], axis=0).T
    sign = jnp.where(lax.broadcasted_iota(jnp.int32, (8, 128), 0) < 4, -1.0, 1.0)
    plain = [stacked[8 * t : 8 * t + 8] for t in range(pairs)]
    swapped = [pltpu.roll(x, 4, 0) * sign for x in plain]
    phase_cos = [[phase_cos_ref[t * blocks + b : t * blocks + b + 1, :] for t in range(pairs)] for b in range(used)]
    phase_sin = [[phase_sin_ref[t * blocks + b : t * blocks + b + 1, :] for t in range(pairs)] for b in range(used)]
    turned = jnp.concatenate(
        [
            jnp.concatenate(
                [plain[t] * phase_cos[b][t] + swapped[t] * phase_sin[b][t] for t in range(pairs)], axis=1
            )
            for b in range(used)
        ],
        axis=0,
    )
    table_high = table_high_ref[...]
    table_low = table_low_ref[...]
    grid = three_products(turned, table_high, table_low, dot_nn)
    zonal_factor = factor_ref[0:8, :]
    merid_factor = factor_ref[8:16, :]
    vertical_factor = factor_ref[16:24, :]
    lane = lax.broadcasted_iota(jnp.int32, (8, 128), 1)
    east, other, merid = [], [], []
    for b in range(used):
        q = q_ref[pl.ds(b, 8, stride=used), :]
        above = above_ref[pl.ds(b, 8, stride=used), :]
        below = below_ref[pl.ds(b, 8, stride=used), :]
        above, below = jnp.where(even, above, below), jnp.where(even, below, above)
        field = grid[8 * b : 8 * b + 4, 0:128] + grid[8 * b + 4 : 8 * b + 8, 128:256]
        east.append(field[0:1] * q)
        merid.append(field[1:2] * q)
        other.append((field[3:4] * (above - below) - field[2:3] * (q + below)) * vertical_factor)
    ahead = [pltpu.roll(z, 127, 1) for z in east]
    behind = [pltpu.roll(z, 1, 1) for z in east]
    rest = []
    for b in range(used):
        right = jnp.where(lane == 127, ahead[(b + 1) % used], ahead[b])
        left = jnp.where(lane == 0, behind[(b - 1) % used], behind[b])
        rest.append(other[b] + zonal_factor * (right - left))
    values = jnp.concatenate(rest + merid, axis=0)
    along_cos = three_products(values, table_high[:, 0:128], table_low[:, 0:128], dot_nt)
    along_sin = three_products(values, table_high[:, 128:256], table_low[:, 128:256], dot_nt)
    for kind in range(2):
        stack = []
        for t in range(pairs):
            cos_total = jnp.zeros((8, 128), f32)
            sin_total = jnp.zeros((8, 128), f32)
            for b in range(used):
                row = 8 * (kind * used + b)
                c = along_cos[row : row + 8, 128 * t : 128 * t + 128]
                s = along_sin[row : row + 8, 128 * t : 128 * t + 128]
                cos_total = cos_total + phase_cos[b][t] * c + phase_sin[b][t] * s
                sin_total = sin_total + phase_cos[b][t] * s - phase_sin[b][t] * c
            stack += [cos_total, sin_total]
        stack += [merid_factor] * (16 - 2 * pairs)
        sent = jnp.concatenate(stack, axis=0).T
        for parity in range(2):
            out_ref[pl.ds(kind * 2 + parity, waves, stride=4), :] = sent[parity * 64 : parity * 64 + waves]


def result_kernel(got_ref, high_ref, low_ref, out_ref):
    degrees = high_ref.shape[1]
    rows = got_ref.shape[0] // 4
    slots = high_ref.shape[0] // rows
    tiles = degrees // 128
    zero_row = jnp.zeros((1, 128), f32)
    parts = []
    for parity in range(2):
        rest = got_ref[pl.ds(parity, rows, stride=4), :]
        merid = got_ref[pl.ds(2 + parity, rows, stride=4), :]
        factor = rest[:, 80:81]
        north = jnp.concatenate([merid[1:], zero_row], axis=0)
        south = jnp.concatenate([zero_row, merid[:-1]], axis=0)
        parts.append(rest + factor * (north - south))
    stacked = jnp.concatenate(parts, axis=0).T
    first = lax.broadcasted_iota(jnp.int32, (16, 2 * rows), 1) < rows
    for t in range(slots // 2):
        block = stacked[16 * t : 16 * t + 16]
        left = jnp.concatenate([jnp.where(first, block, 0.0), jnp.where(first, 0.0, block)], axis=0)
        pair = slice(2 * t * rows, 2 * (t + 1) * rows)
        product = three_products(left, high_ref[pair, :], low_ref[pair, :], dot_nn)
        for parity in range(2):
            s = 2 * t + parity
            for part in range(2):
                row = parity * 16 + part * 8
                kept = product[row : row + 8]
                for tile in range(tiles):
                    start = (part * slots + s) * tiles + tile
                    out_ref[pl.ds(start, 8, stride=2 * slots * tiles), :] = kept[:, 128 * tile : 128 * tile + 128]


def local(x):
    return x if INTERPRET else pltpu.with_memory_space_constraint(x, pltpu.VMEM)


def shaped(shape, dtype=f32):
    return jax.ShapeDtypeStruct(shape, dtype) if INTERPRET else pltpu.VMEM(shape, dtype)


def shards(vort_div, legendre, owner_map, lat_sine, quad_weight, thickness, tracers):
    slots, rows, degrees = legendre.shape
    waves = lax.axis_size("wave")
    levels = lax.axis_size("lev")
    count, _, _, length = tracers.shape
    call = lambda kernel, **kw: pl.pallas_call(kernel, interpret=INTERPRET, **kw)
    swaps = []
    for first in range(2):
        pairs = [(i, i + 1) for i in range(first, levels - 1, 2)]
        swaps.append(lax.ppermute(tracers, "lev", pairs + [(b, a) for a, b in pairs]))
    owner = owner_map
    if INTERPRET:
        owner = jnp.concatenate([owner_map, lax.axis_index("wave").reshape(1)])
    depth = levels // 2
    columns = [[half * depth + z for z in range(depth)] for half in range(2)]
    planes = [
        [w * levels + half * depth + z for half in range(2) for w in range(waves)] for z in range(depth)
    ]
    level = (lax.axis_index("lev").reshape(1),) if INTERPRET else ()
    fourier, message, leg_high, leg_low = call(
        winds_kernel,
        name="winds",
        in_specs=[hbm, hbm, hbm, hbm],
        out_specs=(vmem, vmem, vmem, vmem),
        out_shape=(
            shaped((4 * slots, 128)),
            shaped((depth * slots, 128)),
            shaped((slots * rows, degrees), bf16),
            shaped((slots * rows, degrees), bf16),
        ),
        scratch_shapes=[
            pltpu.VMEM((4 * slots * degrees // 128, 128), f32),
            pltpu.VMEM((slots, rows, degrees), f32),
            pltpu.SMEM(owner.shape, jnp.int32),
            pltpu.SMEM((1, 1), f32),
            pltpu.VMEM((degrees, 128), f32),
            pltpu.VMEM((slots, 128), f32),
            pltpu.SemaphoreType.DMA((4,)),
        ],
    )(vort_div.reshape(4 * slots * degrees // 128, 128), legendre, owner, thickness.reshape(1, 1))
    totals = lax.all_to_all(
        message.reshape(depth, 1, slots * 128),
        "lev",
        split_axis=0,
        concat_axis=0,
        tiled=True,
        axis_index_groups=columns,
    ).reshape(depth * slots, 128)
    table_high, table_low, phase_cos, phase_sin, factors = call(
        table_kernel,
        name="tables",
        in_specs=[vmem, smem, smem, smem],
        out_specs=(vmem, vmem, vmem, vmem, vmem),
        out_shape=(
            shaped((waves * slots, 256), bf16),
            shaped((waves * slots, 256), bf16),
            shaped((slots // 2 * 16, 128)),
            shaped((slots // 2 * 16, 128)),
            shaped((24, 128)),
        ),
    )(local(owner_map.reshape(waves, slots)), lat_sine, quad_weight, thickness)
    sent = call(
        prefix_kernel,
        name="prefix",
        in_specs=[vmem, vmem] + [smem] * len(level),
        out_specs=vmem,
        out_shape=shaped((2 * rows, 128)),
        scratch_shapes=[pltpu.VMEM((256, 128), f32)],
    )(local(totals), local(fourier), *level)
    got = lax.all_to_all(
        sent.reshape(2 * rows, 1, 128),
        ("wave", "lev"),
        split_axis=0,
        concat_axis=0,
        tiled=True,
        axis_index_groups=planes,
    ).reshape(2 * waves, 128)
    flat = lambda x: local(x.reshape(count * length // 128, 128))
    spectra = call(
        grid_kernel,
        name="grid",
        in_specs=[vmem] * 9 + [smem] * len(level),
        out_specs=vmem,
        out_shape=shaped((waves * 4, 128)),
    )(
        local(got),
        local(table_high),
        local(table_low),
        local(phase_cos),
        local(phase_sin),
        flat(tracers),
        flat(swaps[1]),
        flat(swaps[0]),
        local(factors),
        *level,
    )
    back = lax.all_to_all(
        spectra.reshape(waves, 4, 128), "wave", split_axis=0, concat_axis=0, tiled=True
    ).reshape(rows * 4, 128)
    result = call(
        result_kernel,
        name="result",
        in_specs=[vmem, vmem, vmem],
        out_specs=vmem,
        out_shape=jax.ShapeDtypeStruct((count * 2 * slots * degrees // 128, 128), f32),
    )(local(back), local(leg_high), local(leg_low))
    return result.reshape(count, 2, 1, slots, degrees)


def solution(mesh):
    placed = (
        P(None, "lev", "wave", None),
        P("wave", None, None),
        P(),
        P("wave"),
        P("wave"),
        P("lev"),
        P(None, "lev", "wave", None),
    )

    return jax.shard_map(
        shards,
        mesh=mesh,
        in_specs=placed,
        out_specs=P(None, None, "lev", "wave", None),
        check_vma=False,
    )
```

```python
import functools
import math

import jax
import jax.numpy as jnp
from jax import lax
from jax.experimental import pallas as pl
from jax.experimental.pallas import tpu as pltpu
from jax.sharding import PartitionSpec as P


planet_radius = 20.0
INTERPRET = False
f32 = jnp.float32
bf16 = jnp.bfloat16

vmem = pl.BlockSpec(memory_space=pltpu.VMEM)
hbm = pl.BlockSpec(memory_space=pltpu.HBM)
smem = pl.BlockSpec(memory_space=pltpu.SMEM)


def halves(x):
    high = x.astype(bf16)
    low = (x - high.astype(f32)).astype(bf16)
    return high, low


def dot_nn(left, right):
    return lax.dot_general(left, right, (((1,), (0,)), ((), ())), preferred_element_type=f32)


def dot_nt(left, right):
    return lax.dot_general(left, right, (((1,), (1,)), ((), ())), preferred_element_type=f32)


def three_products(left, right_high, right_low, dot):
    rows = left.shape[0]
    high, low = halves(left)
    both = dot(jnp.concatenate([high, low], axis=0), right_high)
    return both[:rows] + both[rows:] + dot(high, right_low)


def cos_sin(steps, quarter):
    turns = jnp.floor(steps * (1.0 / quarter) + 0.5)
    angle = (steps - turns * quarter) * (0.5 * math.pi / quarter)
    z = angle * angle
    sine = ((-1.9515295891e-4 * z + 8.3321608736e-3) * z - 1.6666654611e-1) * z * angle + angle
    cosine = (
        (2.443315711809948e-5 * z - 1.388731625493765e-3) * z + 4.166664568298827e-2
    ) * z * z - 0.5 * z + 1.0
    turn = turns.astype(jnp.int32)
    odd = (turn & 1) == 1
    first = jnp.where(odd, sine, cosine)
    second = jnp.where(odd, cosine, sine)
    return (
        jnp.where(((turn + 1) & 2) == 2, -first, first),
        jnp.where((turn & 2) == 2, -second, second),
    )


def own_orders(owner_ref, slots):
    start = lax.axis_index("wave") * slots if not INTERPRET else owner_ref[owner_ref.shape[0] - 1] * slots
    return [owner_ref[start + s] for s in range(slots)]


def winds_kernel(
    vort_hbm,
    leg_hbm,
    owner_hbm,
    thick_hbm,
    f_ref,
    lev_ref,
    high_ref,
    low_ref,
    vort_ref,
    leg_ref,
    owner_ref,
    thick_ref,
    field_ref,
    msg_ref,
    sem,
):
    slots, rows, degrees = leg_ref.shape
    copies = lev_ref.shape[0] // slots
    tiles = degrees // 128
    vort_copy = pltpu.make_async_copy(vort_hbm, vort_ref, sem.at[0])
    owner_copy = pltpu.make_async_copy(owner_hbm, owner_ref, sem.at[1])
    thick_copy = pltpu.make_async_copy(thick_hbm, thick_ref, sem.at[2])
    owner_copy.start(priority=1)
    thick_copy.start(priority=1)
    vort_copy.start(priority=1)

    leg_copy = pltpu.make_async_copy(leg_hbm, leg_ref, sem.at[3])
    leg_copy.start()
    owner_copy.wait()
    own = own_orders(owner_ref, slots)
    row = lax.broadcasted_iota(jnp.int32, (slots, degrees), 0)
    order = jnp.zeros((slots, degrees), f32)
    for s in range(slots):
        order = jnp.where(row == s, own[s].astype(f32), order)

    def vort(part):
        start = part * slots * tiles
        return jnp.concatenate(
            [vort_ref[pl.ds(start + tile, slots, stride=tiles), :] for tile in range(tiles)], axis=1
        )

    degree = lax.broadcasted_iota(jnp.int32, (slots, degrees), 1).astype(f32)

    def coupling_at(n):
        ratio = jnp.maximum(n * n - order * order, 0.0) / jnp.maximum(4.0 * n * n - 1.0, 1.0)
        return jnp.where(n > order, jnp.sqrt(ratio), 0.0)

    coupling = coupling_at(degree)
    last = degree == degrees - 1
    coupling_next = jnp.where(last, 0.0, coupling_at(degree + 1.0))
    lower_factor = -(degree - 1.0) * coupling
    upper_factor = (degree + 2.0) * coupling_next
    inverse = jnp.where(
        degree > 0, -planet_radius * planet_radius / jnp.maximum(degree * (degree + 1.0), 1.0), 0.0
    )
    valid = degree >= order

    def derivative(field):
        lower = jnp.where(degree == 0, 0.0, pltpu.roll(field, 1, 1))
        upper = jnp.where(last, 0.0, pltpu.roll(field, degrees - 1, 1))
        return lower_factor * lower + upper_factor * upper

    vort_copy.wait()
    thick_copy.wait()
    leg_copy.wait()
    div_real = vort(2)
    div_imag = vort(3)
    stream_real = inverse * vort(0)
    stream_imag = inverse * vort(1)
    potential_real = inverse * div_real
    potential_imag = inverse * div_imag
    scale = 1.0 / planet_radius
    thickness = thick_ref[0, 0]
    zeros = jnp.zeros((slots, degrees), f32)
    fields = [
        (-order * potential_imag - derivative(stream_real)) * scale,
        (-order * stream_imag + derivative(potential_real)) * scale,
        div_real * thickness,
        zeros,
        (order * potential_real - derivative(stream_imag)) * scale,
        (order * stream_real + derivative(potential_imag)) * scale,
        div_imag * thickness,
        zeros,
    ]
    for f, field in enumerate(fields):
        for tile in range(tiles):
            start = 128 * tile + 16 * f
            field_ref[start : start + slots, :] = field[:, 128 * tile : 128 * tile + 128]
    first = lax.broadcasted_iota(jnp.int32, (8, 2 * rows), 1) < rows
    for t in range(slots // 2):
        blocks = [
            jnp.concatenate(
                [
                    field_ref[pl.ds(128 * tile + 2 * t + parity, 8, stride=16), :]
                    for tile in range(tiles)
                ],
                axis=1,
            )
            for parity in range(2)
        ]
        left = jnp.concatenate(blocks, axis=0)
        left_low = left - left.astype(bf16).astype(f32)
        left = jnp.concatenate([left, left_low], axis=0).astype(bf16)
        highs, lows = [], []
        for parity in range(2):
            s = 2 * t + parity
            leg_high, leg_low = halves(jnp.where(valid[s : s + 1], leg_ref[s], 0.0))
            high_ref[s * rows : (s + 1) * rows, :] = leg_high
            low_ref[s * rows : (s + 1) * rows, :] = leg_low
            highs.append(leg_high)
            lows.append(leg_low)
        product = dot_nt(left, jnp.concatenate(highs + lows, axis=0))
        total = product[0:16, 0:128] + product[0:16, 128:256] + product[16:32, 0:128]
        total = jnp.where(first, total[0:8], total[8:16])
        f_ref[8 * t : 8 * t + 8, :] = total
        msg_ref[2 * t : 2 * t + 1, :] = total[2:3]
        msg_ref[2 * t + 1 : 2 * t + 2, :] = total[6:7]
    message = msg_ref[...]
    for copy in range(copies):
        lev_ref[copy * slots : (copy + 1) * slots, :] = message


def table_kernel(
    owner_ref,
    sine_ref,
    weight_ref,
    thick_ref,
    table_high_ref,
    table_low_ref,
    phase_cos_ref,
    phase_sin_ref,
    factor_ref,
):
    waves, slots = owner_ref.shape
    length = 2.0 * waves * slots
    orders = owner_ref[...].astype(f32)
    offset = lax.broadcasted_iota(jnp.int32, (waves, 128), 1).astype(f32)
    padded = jnp.concatenate([orders, jnp.zeros((waves, 128 - slots), f32)], axis=1)
    by_slot = padded.T
    blocks = phase_cos_ref.shape[0] // (slots // 2)
    block = lax.broadcasted_iota(jnp.int32, (blocks, 128), 0).astype(f32)
    for s in range(slots):
        cosine, sine = cos_sin(orders[:, s : s + 1] * offset, length / 4.0)
        cos_high, cos_low = halves(cosine)
        sin_high, sin_low = halves(-sine)
        rows = slice(s * waves, (s + 1) * waves)
        table_high_ref[rows, 0:128] = cos_high
        table_high_ref[rows, 128:256] = sin_high
        table_low_ref[rows, 0:128] = cos_low
        table_low_ref[rows, 128:256] = sin_low
    for t in range(slots // 2):
        row = jnp.concatenate([by_slot[2 * t : 2 * t + 1, :], by_slot[2 * t + 1 : 2 * t + 2, :]], axis=1)
        cosine, sine = cos_sin(row * block * 128.0, length / 4.0)
        phase_cos_ref[t * blocks : (t + 1) * blocks, :] = cosine
        phase_sin_ref[t * blocks : (t + 1) * blocks, :] = sine
    step = 2.0 * math.pi / length
    sine = sine_ref[0]
    weight = jnp.full((8, 128), -weight_ref[0] * (2.0 / length), f32)
    slope = weight / ((1.0 - sine * sine) * (2.0 * step))
    factor_ref[0:8, :] = slope
    factor_ref[8:16, :] = slope
    factor_ref[16:24, :] = weight / (2.0 * thick_ref[0])


def prefix_kernel(got_ref, f_ref, *rest):
    level_ref, out_ref, ft_ref = rest if INTERPRET else (None, *rest)
    level = level_ref[0] if INTERPRET else lax.axis_index("lev")
    pairs = f_ref.shape[0] // 8
    depth = got_ref.shape[0] // (2 * pairs)
    half = level // depth
    own_sum = jnp.zeros((2 * pairs, 128), f32)
    all_sum = jnp.zeros((2 * pairs, 128), f32)
    for source in range(depth):
        part = got_ref[source * 2 * pairs : (source + 1) * 2 * pairs, :]
        own_sum = own_sum + jnp.where(source < level - half * depth, part, 0.0)
        all_sum = all_sum + part
    to_upper = jnp.where(half == 0, all_sum, 0.0)
    blocks = []
    for block, total in enumerate((own_sum, to_upper)):
        start = 128 * block
        if block == 0:
            ft_ref[start : start + 8 * pairs, :] = f_ref[...]
            ft_ref[start + 8 * pairs : start + 128, :] = jnp.zeros((128 - 8 * pairs, 128), f32)
        else:
            ft_ref[start : start + 128, :] = jnp.zeros((128, 128), f32)
        for t in range(pairs):
            row = start + 8 * t
            ft_ref[row + 3 : row + 4, :] = total[2 * t : 2 * t + 1]
            ft_ref[row + 7 : row + 8, :] = total[2 * t + 1 : 2 * t + 2]
        turned = ft_ref[start : start + 128, :].T
        blocks.append(turned[0:64] + pltpu.roll(turned[64:128], 64, 1))
    own_block, other_block = blocks
    out_ref[0:64, :] = jnp.where(half == 0, own_block, other_block)
    out_ref[64:128, :] = jnp.where(half == 0, other_block, own_block)


def grid_kernel(
    got_ref,
    table_high_ref,
    table_low_ref,
    phase_cos_ref,
    phase_sin_ref,
    q_ref,
    above_ref,
    below_ref,
    far_ref,
    factor_ref,
    *rest,
    depth,
):
    level_ref, out_ref = rest if INTERPRET else (None, *rest)
    level = level_ref[0] if INTERPRET else lax.axis_index("lev")
    first_level = level % depth == 0
    last_level = level % depth == depth - 1
    waves = got_ref.shape[0] // 2
    pairs = 5
    blocks = phase_cos_ref.shape[0] // pairs
    used = q_ref.shape[0] // 8
    got = got_ref[0:waves, :] + got_ref[waves : 2 * waves, :]
    stacked = jnp.concatenate([got, pltpu.roll(got, 64, 1)], axis=0).T
    sign = jnp.where(lax.broadcasted_iota(jnp.int32, (8, 128), 0) < 4, -1.0, 1.0)
    plain = [stacked[8 * t : 8 * t + 8] for t in range(pairs)]
    swapped = [pltpu.roll(x, 4, 0) * sign for x in plain]
    phase_cos = [[phase_cos_ref[t * blocks + b : t * blocks + b + 1, :] for t in range(pairs)] for b in range(used)]
    phase_sin = [[phase_sin_ref[t * blocks + b : t * blocks + b + 1, :] for t in range(pairs)] for b in range(used)]
    turned = jnp.concatenate(
        [
            jnp.concatenate(
                [plain[t] * phase_cos[b][t] + swapped[t] * phase_sin[b][t] for t in range(pairs)], axis=1
            )
            for b in range(used)
        ],
        axis=0,
    )
    table_high = table_high_ref[...]
    table_low = table_low_ref[...]
    grid = three_products(turned, table_high, table_low, dot_nn)
    zonal_factor = factor_ref[0:8, :]
    merid_factor = factor_ref[8:16, :]
    vertical_factor = factor_ref[16:24, :]
    lane = lax.broadcasted_iota(jnp.int32, (8, 128), 1)
    east, other, merid = [], [], []
    for b in range(used):
        q = q_ref[pl.ds(b, 8, stride=used), :]
        above = above_ref[pl.ds(b, 8, stride=used), :]
        below = below_ref[pl.ds(b, 8, stride=used), :]
        far = far_ref[pl.ds(b, 8, stride=used), :]
        above = jnp.where(first_level, far, above)
        below = jnp.where(last_level, far, below)
        field = grid[8 * b : 8 * b + 4, 0:128] + grid[8 * b + 4 : 8 * b + 8, 128:256]
        east.append(field[0:1] * q)
        merid.append(field[1:2] * q)
        other.append((field[3:4] * (above - below) - field[2:3] * (q + below)) * vertical_factor)
    ahead = [pltpu.roll(z, 127, 1) for z in east]
    behind = [pltpu.roll(z, 1, 1) for z in east]
    rest = []
    for b in range(used):
        right = jnp.where(lane == 127, ahead[(b + 1) % used], ahead[b])
        left = jnp.where(lane == 0, behind[(b - 1) % used], behind[b])
        rest.append(other[b] + zonal_factor * (right - left))
    values = jnp.concatenate(rest + merid, axis=0)
    along_cos = three_products(values, table_high[:, 0:128], table_low[:, 0:128], dot_nt)
    along_sin = three_products(values, table_high[:, 128:256], table_low[:, 128:256], dot_nt)
    for kind in range(2):
        stack = []
        for t in range(pairs):
            cos_total = jnp.zeros((8, 128), f32)
            sin_total = jnp.zeros((8, 128), f32)
            for b in range(used):
                row = 8 * (kind * used + b)
                c = along_cos[row : row + 8, 128 * t : 128 * t + 128]
                s = along_sin[row : row + 8, 128 * t : 128 * t + 128]
                cos_total = cos_total + phase_cos[b][t] * c + phase_sin[b][t] * s
                sin_total = sin_total + phase_cos[b][t] * s - phase_sin[b][t] * c
            stack += [cos_total, sin_total]
        stack += [merid_factor] * (16 - 2 * pairs)
        sent = jnp.concatenate(stack, axis=0).T
        for parity in range(2):
            out_ref[pl.ds(kind * 2 + parity, waves, stride=4), :] = sent[parity * 64 : parity * 64 + waves]


def result_kernel(got_ref, high_ref, low_ref, out_ref):
    degrees = high_ref.shape[1]
    rows = got_ref.shape[0] // 4
    slots = high_ref.shape[0] // rows
    tiles = degrees // 128
    zero_row = jnp.zeros((1, 128), f32)
    parts = []
    for parity in range(2):
        rest = got_ref[pl.ds(parity, rows, stride=4), :]
        merid = got_ref[pl.ds(2 + parity, rows, stride=4), :]
        factor = rest[:, 80:81]
        north = jnp.concatenate([merid[1:], zero_row], axis=0)
        south = jnp.concatenate([zero_row, merid[:-1]], axis=0)
        parts.append(rest + factor * (north - south))
    stacked = jnp.concatenate(parts, axis=0).T
    first = lax.broadcasted_iota(jnp.int32, (16, 2 * rows), 1) < rows
    for t in range(slots // 2):
        block = stacked[16 * t : 16 * t + 16]
        left = jnp.concatenate([jnp.where(first, block, 0.0), jnp.where(first, 0.0, block)], axis=0)
        pair = slice(2 * t * rows, 2 * (t + 1) * rows)
        product = three_products(left, high_ref[pair, :], low_ref[pair, :], dot_nn)
        for parity in range(2):
            s = 2 * t + parity
            for part in range(2):
                row = parity * 16 + part * 8
                kept = product[row : row + 8]
                for tile in range(tiles):
                    start = (part * slots + s) * tiles + tile
                    out_ref[pl.ds(start, 8, stride=2 * slots * tiles), :] = kept[:, 128 * tile : 128 * tile + 128]


def local(x):
    return x if INTERPRET else pltpu.with_memory_space_constraint(x, pltpu.VMEM)


def shaped(shape, dtype=f32):
    return jax.ShapeDtypeStruct(shape, dtype) if INTERPRET else pltpu.VMEM(shape, dtype)


def shards(vort_div, legendre, owner_map, lat_sine, quad_weight, thickness, tracers):
    slots, rows, degrees = legendre.shape
    waves = lax.axis_size("wave")
    levels = lax.axis_size("lev")
    count, _, _, length = tracers.shape
    call = lambda kernel, **kw: pl.pallas_call(kernel, interpret=INTERPRET, **kw)
    depth = levels // 2
    up = [(h + z, h + z + 1) for h in (0, depth) for z in range(depth - 1)]
    down = [(b, a) for a, b in up]
    far = lax.ppermute(tracers, "lev", [(depth - 1, depth), (depth, depth - 1)])
    above = lax.ppermute(tracers, "lev", up)
    below = lax.ppermute(tracers, "lev", down)
    owner = owner_map
    if INTERPRET:
        owner = jnp.concatenate([owner_map, lax.axis_index("wave").reshape(1)])
    columns = [[half * depth + z for z in range(depth)] for half in range(2)]
    planes = [
        [w * levels + half * depth + z for half in range(2) for w in range(waves)] for z in range(depth)
    ]
    level = (lax.axis_index("lev").reshape(1),) if INTERPRET else ()
    fourier, message, leg_high, leg_low = call(
        winds_kernel,
        name="winds",
        in_specs=[hbm, hbm, hbm, hbm],
        out_specs=(vmem, vmem, vmem, vmem),
        out_shape=(
            shaped((4 * slots, 128)),
            shaped((depth * slots, 128)),
            shaped((slots * rows, degrees), bf16),
            shaped((slots * rows, degrees), bf16),
        ),
        scratch_shapes=[
            pltpu.VMEM((4 * slots * degrees // 128, 128), f32),
            pltpu.VMEM((slots, rows, degrees), f32),
            pltpu.SMEM(owner.shape, jnp.int32),
            pltpu.SMEM((1, 1), f32),
            pltpu.VMEM((degrees, 128), f32),
            pltpu.VMEM((slots, 128), f32),
            pltpu.SemaphoreType.DMA((4,)),
        ],
    )(vort_div.reshape(4 * slots * degrees // 128, 128), legendre, owner, thickness.reshape(1, 1))
    totals = lax.all_to_all(
        message.reshape(depth, 1, slots * 128),
        "lev",
        split_axis=0,
        concat_axis=0,
        tiled=True,
        axis_index_groups=columns,
    ).reshape(depth * slots, 128)
    table_high, table_low, phase_cos, phase_sin, factors = call(
        table_kernel,
        name="tables",
        in_specs=[vmem, smem, smem, smem],
        out_specs=(vmem, vmem, vmem, vmem, vmem),
        out_shape=(
            shaped((waves * slots, 256), bf16),
            shaped((waves * slots, 256), bf16),
            shaped((slots // 2 * 16, 128)),
            shaped((slots // 2 * 16, 128)),
            shaped((24, 128)),
        ),
    )(local(owner_map.reshape(waves, slots)), lat_sine, quad_weight, thickness)
    sent = call(
        prefix_kernel,
        name="prefix",
        in_specs=[vmem, vmem] + [smem] * len(level),
        out_specs=vmem,
        out_shape=shaped((2 * rows, 128)),
        scratch_shapes=[pltpu.VMEM((256, 128), f32)],
    )(local(totals), local(fourier), *level)
    got = lax.all_to_all(
        sent.reshape(2 * rows, 1, 128),
        ("wave", "lev"),
        split_axis=0,
        concat_axis=0,
        tiled=True,
        axis_index_groups=planes,
    ).reshape(2 * waves, 128)
    flat = lambda x: local(x.reshape(count * length // 128, 128))
    spectra = call(
        functools.partial(grid_kernel, depth=depth),
        name="grid",
        in_specs=[vmem] * 10 + [smem] * len(level),
        out_specs=vmem,
        out_shape=shaped((waves * 4, 128)),
    )(
        local(got),
        local(table_high),
        local(table_low),
        local(phase_cos),
        local(phase_sin),
        flat(tracers),
        flat(above),
        flat(below),
        flat(far),
        local(factors),
        *level,
    )
    back = lax.all_to_all(
        spectra.reshape(waves, 4, 128), "wave", split_axis=0, concat_axis=0, tiled=True
    ).reshape(rows * 4, 128)
    result = call(
        result_kernel,
        name="result",
        in_specs=[vmem, vmem, vmem],
        out_specs=vmem,
        out_shape=jax.ShapeDtypeStruct((count * 2 * slots * degrees // 128, 128), f32),
    )(local(back), local(leg_high), local(leg_low))
    return result.reshape(count, 2, 1, slots, degrees)


def solution(mesh):
    placed = (
        P(None, "lev", "wave", None),
        P("wave", None, None),
        P(),
        P("wave"),
        P("wave"),
        P("lev"),
        P(None, "lev", "wave", None),
    )

    return jax.shard_map(
        shards,
        mesh=mesh,
        in_specs=placed,
        out_specs=P(None, None, "lev", "wave", None),
        check_vma=False,
    )
```
